32 devices in a mesh: dp: 8 (over y, x, core), tensor: 4 (over z).
Axes of the slice: x: 2, y: 2, z: 4, core: 2. Of those that a mesh axis runs over, the one named last changes fastest.
Arguments:
- activations: bfloat16 [4096, 8192], P('dp', 'tensor'), may hold values from -6 to 6
- out_grads: bfloat16 [4096, 28672], P('dp', 'tensor'), may hold values from -6 to 6
- input_proj: bfloat16 [8192, 64], P('tensor'), may hold values from -0.0625 to 0.0625
- grad_proj: bfloat16 [28672, 64], P('tensor'), may hold values from -4 to 4, as said below
- example_count: int32 [8], P('dp'), may hold values from 1 to 4, as said below
- child_order: int32 [8], replicated, may hold values 0 or 1
- prior_sketch: float32 [2048, 4096], P('dp', 'tensor'), may hold values from -6 to 6
- fold_map: float32 [256, 4], replicated, may hold values from -3 to 3
- merge_mix: float32 [256, 512], replicated, may hold values from -0.25 to 0.25
Outputs:
- merged_sketch: float32 [256, 4096], P(None, 'tensor')
- preconditioned: float32 [32, 4096], P('dp', 'tensor')
The draws below stay inside these ranges and needn't reach their ends.
Inputs may be any that keep to these rules, and one draw needn't show every extreme that they name: `example_count`: some data rank has exactly 4 live examples. `grad_proj`: entries within 26 / sqrt(28672) of zero.
All inputs are finite; a program needn't handle non-finite values.
Results may differ from the reference program's by a relative error of at most 0.0003.
Values sent between devices are 32-bit elements; how exact they have to be, the bound alone decides.
A program may use at most 64 MiB of HBM per device.

```python
import jax
import jax.numpy as jnp
import numpy as np
from jax import lax

D = 8192
FF = 28672
RANK = 64
PROJ = 4096
SKETCH = 256
SEQ = 128
EX_DEV = 4
EXAMPLES = 32
TOKENS = 4096
LEVELS = 3
N_DP = 8


def draw_grad_proj(key, part):
    key_base, key_jitter = jax.random.split(key, 2)
    base = jnp.clip(jax.random.normal(key_base, (FF, RANK), jnp.float32), -6.0, 6.0)
    rising = jnp.exp(jnp.log(3.0) * jnp.arange(RANK, dtype=jnp.float32) / (RANK - 1))
    jitter = jax.random.uniform(key_jitter, (RANK,), jnp.float32, 0.7, 1.4)
    return (base * rising * jitter / jnp.sqrt(jnp.float32(FF))).astype(jnp.bfloat16)


def draw_example_count(key, part):
    key_counts, key_pick = jax.random.split(jax.random.fold_in(key, 11), 2)
    counts = jax.random.randint(key_counts, (N_DP,), 1, EX_DEV + 1, dtype=jnp.int32)
    chosen = jax.random.randint(key_pick, (), 0, N_DP, dtype=jnp.int32)
    positions = jnp.arange(N_DP, dtype=jnp.int32)
    return jnp.where(positions == chosen, EX_DEV, counts).astype(jnp.int32)


def touch_ends(values, key, least, top_value):
    index_at = [jax.random.randint(jax.random.fold_in(key, axis), (), 0, length) for axis, length in enumerate(values.shape)]
    widest = values.shape.index(max(values.shape))
    next_to = index_at[:widest] + [(index_at[widest] + 1) % values.shape[widest]] + index_at[widest + 1:]
    return values.at[tuple(index_at)].set(least).at[tuple(next_to)].set(top_value)


def block_scale(rng, extent, shards, low, top_value):
    factor_of, own = 1.0, jax.random.fold_in(rng, 6)
    for axis_at, parts in shards:
        heights = jnp.exp(jax.random.uniform(jax.random.fold_in(own, axis_at), (parts,), jnp.float32, low / len(shards), top_value / len(shards)))
        factor_of = factor_of * jnp.repeat(heights, extent[axis_at] // parts).reshape([-1 if axis == axis_at else 1 for axis in range(len(extent))])
    return factor_of


def bell_draw(own_key, shape, width, bound, cuts=(), kind=jnp.bfloat16):
    result = width * jax.random.normal(own_key, shape, jnp.float32)
    if cuts:
        result = result * block_scale(own_key, shape, cuts, -0.22, 0.18)
    return jnp.clip(result, -bound, bound).astype(kind)


def setup_inputs(seed: int = 0) -> dict:
    key_of = jax.random.split(jax.random.key(seed), 10)
    return {
        "activations": bell_draw(key_of[0], (TOKENS, D), 1.0, 6.0, ((0, 8), (1, 4))),
        "out_grads": bell_draw(key_of[1], (TOKENS, FF), 1.0, 6.0, ((0, 8), (1, 4))),
        "input_proj": bell_draw(key_of[2], (D, RANK), D ** -0.5, 0.0625, ((0, 4),)),
        "grad_proj": draw_grad_proj(jax.random.fold_in(key_of[9], 71), 0),
        "example_count": draw_example_count(jax.random.fold_in(key_of[9], 71), 0),
        "child_order": touch_ends((jax.random.randint(key_of[5], (N_DP,), 0, 2) < 1).astype(jnp.int32), jax.random.fold_in(key_of[5], 1), 0, 1),
        "prior_sketch": bell_draw(key_of[6], (N_DP * SKETCH, PROJ), 1.0, 6.0, ((0, 8), (1, 4)), jnp.float32),
        "fold_map": bell_draw(key_of[7], (SKETCH, EX_DEV), EX_DEV ** -0.5, 3.0, (), jnp.float32),
        "merge_mix": bell_draw(key_of[8], (SKETCH, 2 * SKETCH), (2 * SKETCH) ** -0.5, 0.25, (), jnp.float32),
    }


def reference(activations, out_grads, input_proj, grad_proj, example_count, child_order, prior_sketch, fold_map, merge_mix):
    input_side = jnp.dot(activations.astype(jnp.float32), input_proj.astype(jnp.float32), preferred_element_type=jnp.float32)
    grad_side = jnp.dot(out_grads.astype(jnp.float32), grad_proj.astype(jnp.float32), preferred_element_type=jnp.float32)
    grad_blocks = grad_side.reshape(EXAMPLES, SEQ, RANK)
    input_blocks = input_side.reshape(EXAMPLES, SEQ, RANK)
    example_grad = jnp.einsum('eta,etb->eab', grad_blocks, input_blocks, precision=lax.Precision.HIGHEST)
    example_grad = example_grad.reshape(EXAMPLES, PROJ) / jnp.sqrt(jnp.float32(SEQ))
    slot_index = jnp.arange(EXAMPLES, dtype=jnp.int32)
    live = slot_index % EX_DEV < example_count[slot_index // EX_DEV]
    example_grad = jnp.where(live[:, None], example_grad, jnp.zeros_like(example_grad))
    grouped = example_grad.reshape(N_DP, EX_DEV, PROJ)
    nodes = prior_sketch.reshape(N_DP, SKETCH, PROJ) + jnp.einsum('sk,nkp->nsp', fold_map, grouped, precision=lax.Precision.HIGHEST)
    masses = lax.optimization_barrier(jnp.sum(nodes * nodes, axis=(1, 2)))
    mix_first = merge_mix[:, :SKETCH]
    mix_second = merge_mix[:, SKETCH:]
    for level_index in range(LEVELS):
        count_pairs = nodes.shape[0] // 2
        flag_index = np.arange(count_pairs) * 2 ** (level_index + 1) + 2 ** level_index - 1
        flips = child_order[flag_index] == 1
        lower_nodes = nodes[0::2]
        upper_nodes = nodes[1::2]
        first = jnp.where(flips[:, None, None], upper_nodes, lower_nodes)
        second = jnp.where(flips[:, None, None], lower_nodes, upper_nodes)
        first_mass = jnp.where(flips, masses[1::2], masses[0::2])
        second_mass = jnp.where(flips, masses[0::2], masses[1::2])
        mixture = jnp.einsum('sk,nkp->nsp', mix_first, first, precision=lax.Precision.HIGHEST) + jnp.einsum('sk,nkp->nsp', mix_second, second, precision=lax.Precision.HIGHEST)
        mix_total = lax.optimization_barrier(jnp.sum(mixture * mixture, axis=(1, 2)))
        masses = first_mass + second_mass
        nodes = mixture * jnp.sqrt(masses / (mix_total + 1e-06))[:, None, None]
    merged_sketch = nodes[0]
    gram = jnp.dot(merged_sketch, merged_sketch.T, precision=lax.Precision.HIGHEST)
    damping = jnp.trace(gram) / SKETCH
    system = gram + damping * jnp.eye(SKETCH, dtype=jnp.float32)
    sketch_grad = jnp.dot(merged_sketch, example_grad.T, precision=lax.Precision.HIGHEST)
    solved = jnp.linalg.solve(system, sketch_grad)
    preconditioned = example_grad - jnp.dot(solved.T, merged_sketch, precision=lax.Precision.HIGHEST)
    return (merged_sketch, preconditioned)
```

```python
import functools

import jax
import jax.numpy as jnp
from jax import lax
from jax.experimental import pallas as pl
from jax.experimental.pallas import tpu as pltpu
from jax.sharding import PartitionSpec as P

RANK = 64
SEQ = 128
LANES = 128
HIGHEST = lax.Precision.HIGHEST
MESH = pl.DeviceIdType.MESH


def newton_plan(rows):
    low, high = 0.999, (rows + 1) * 1.001
    first = 2.0 / (low + high)
    reach, scales = first * low, []
    while 1.0 - reach > 1e-4:
        grown = reach * (2.0 - reach)
        scale = 2.0 / (1.0 + grown)
        scales.append(scale)
        reach = grown * scale
    return first, scales


def dot_high(left, right):
    return jnp.dot(left, right, precision=HIGHEST, preferred_element_type=jnp.float32)


def dot_rows(left, right):
    return lax.dot_general(
        left, right, (((1,), (1,)), ((), ())), precision=HIGHEST, preferred_element_type=jnp.float32
    )


def fused_kernel(
    n_dp,
    n_tp,
    act_hbm,
    out_hbm,
    wi_hbm,
    wo_hbm,
    count_ref,
    order_ref,
    prior_hbm,
    fold_ref,
    mix_ref,
    root_out,
    pre_out,
    act,
    outg,
    wi,
    wo,
    prior,
    zsend,
    zrecv,
    full,
    grads,
    grads_by_tile,
    grads_all,
    sums_z,
    sums_p,
    root,
    gram_part,
    gram_rs,
    gram_z,
    gram,
    rhs,
    pre,
    load_sem,
    prior_send,
    prior_recv,
    z_send,
    z_recv,
    p_send,
    p_recv,
    out_sem,
):
    f32 = jnp.float32
    me, z = lax.axis_index("dp"), lax.axis_index("tensor")
    rows = gram.shape[0]
    block = rows // n_dp
    levels = n_dp.bit_length() - 1

    def dp_of(k):
        return lax.rem(me + k, n_dp)

    def tp_of(k):
        return lax.rem(z + k, n_tp)

    order = sorted(range(1, n_tp), key=lambda k: -min(k, n_tp - k)) + [0]
    loads = []
    for index, (src, dst) in enumerate(((wi_hbm, wi), (wo_hbm, wo))):
        loads.append(pltpu.make_async_copy(src, dst, load_sem.at[index]))
        loads[-1].start()
    chunk_loads = []
    for index, k in enumerate(order):
        e = tp_of(k)
        span = pl.ds(pl.multiple_of(e * SEQ, SEQ), SEQ)
        pair = (
            pltpu.make_async_copy(act_hbm.at[span], act.at[index], load_sem.at[2 + 2 * index]),
            pltpu.make_async_copy(out_hbm.at[span], outg.at[index], load_sem.at[3 + 2 * index]),
        )
        for copy in pair:
            copy.start()
        chunk_loads.append(pair)

    def tile_of(owner):
        return pl.ds(pl.multiple_of(owner * LANES, LANES), LANES)

    own_prior = pltpu.make_async_copy(
        prior_hbm.at[:, tile_of(me)], prior.at[me], load_sem.at[2 + 2 * n_tp]
    )
    own_prior.start()

    barrier = pltpu.get_barrier_semaphore()
    for k in range(1, n_dp):
        pl.semaphore_signal(barrier, inc=1, device_id={"dp": dp_of(k)}, device_id_type=MESH)
    for k in range(1, n_tp):
        pl.semaphore_signal(barrier, inc=1, device_id={"tensor": tp_of(k)}, device_id_type=MESH)
    pl.semaphore_wait(barrier, n_dp + n_tp - 2)

    prior_copies = []
    for k in range(1, n_dp):
        prior_copies.append(
            pltpu.make_async_remote_copy(
                src_ref=prior_hbm.at[:, tile_of(dp_of(k))],
                dst_ref=prior.at[me],
                send_sem=prior_send.at[k],
                recv_sem=prior_recv.at[k],
                device_id={"dp": dp_of(k)},
                device_id_type=MESH,
            )
        )
        prior_copies[-1].start()

    def exchange(axis, phase, source, target):
        size, other = (n_tp, tp_of) if axis == "tensor" else (n_dp, dp_of)
        send, recv = (z_send, z_recv) if axis == "tensor" else (p_send, p_recv)
        copies = []
        for k in range(1, size):
            copies.append(
                pltpu.make_async_remote_copy(
                    src_ref=source(other(k)),
                    dst_ref=target,
                    send_sem=send.at[phase, k],
                    recv_sem=recv.at[phase, k],
                    device_id={axis: other(k)},
                    device_id_type=MESH,
                )
            )
            copies[-1].start()
        return copies

    for copy in loads:
        copy.wait()
    side_copies = []
    for index, k in enumerate(order):
        for copy in chunk_loads[index]:
            copy.wait()
        left = jnp.dot(act[index], wi[...], preferred_element_type=f32)
        right = jnp.dot(outg[index], wo[...], preferred_element_type=f32)
        both = jnp.concatenate([left, right], axis=1)
        if k == 0:
            zrecv[z] = both
        else:
            zsend[index] = both
            copy = pltpu.make_async_remote_copy(
                src_ref=zsend.at[index],
                dst_ref=zrecv.at[z],
                send_sem=z_send.at[0, k],
                recv_sem=z_recv.at[0, k],
                device_id={"tensor": tp_of(k)},
                device_id_type=MESH,
            )
            copy.start()
            side_copies.append(copy)
    for copy in side_copies:
        copy.wait()
    sides = zrecv[0]
    for index in range(1, n_tp):
        sides = sides + zrecv[index]
    lane = lax.broadcasted_iota(jnp.int32, sides.shape, 1)
    doubled = jnp.where(lane < RANK, sides, pltpu.roll(sides, RANK, 1))
    product = dot_high(sides.T, doubled) / jnp.sqrt(f32(SEQ))
    product = jnp.where(z < count_ref[0], product, jnp.zeros_like(product))
    full[...] = product[RANK:]
    even = full[pl.ds(0, RANK // 2, stride=2), :]
    odd = full[pl.ds(1, RANK // 2, stride=2), :]
    lane = lax.broadcasted_iota(jnp.int32, even.shape, 1)
    mine = jnp.where(lane < RANK, even, odd)
    for index in range(n_tp):
        zsend[n_tp + index, 0:n_dp, :] = mine[index * n_dp : (index + 1) * n_dp]
    grads[z] = zsend[n_tp + z, 0:n_dp, :]
    for copy in exchange("tensor", 1, lambda t: zsend.at[n_tp + t, 0:n_dp, :], grads.at[z]):
        copy.wait()
    for index in range(n_tp):
        value = grads[index]
        for tile in range(n_dp):
            grads_by_tile[tile, index : index + 1, :] = value[tile : tile + 1]
    grads_all[me] = grads_by_tile[me]
    grad_copies = exchange("dp", 0, lambda t: grads_by_tile.at[t], grads_all.at[me])
    own_prior.wait()
    for copy in prior_copies:
        copy.wait()
    for copy in grad_copies:
        copy.wait()

    fold = fold_ref[...]
    sums = []

    def total(value):
        sums.append(jnp.sum(jnp.sum(value, axis=0, keepdims=True), axis=1, keepdims=True))
        return len(sums) - 1

    leaves, leaf_mass = [], []
    for r in range(n_dp):
        leaf = prior[r]
        step = grads_all[r]
        for e in range(n_tp):
            leaf = leaf + fold[:, e : e + 1] * step[e : e + 1, :]
        leaf_mass.append(total(leaf * leaf))
        leaves.append([leaf])
    first_mix, second_mix = mix_ref[:, :rows], mix_ref[:, rows:]
    nodes, products, flags = leaves, [], []
    for level in range(levels):
        merged, level_products, level_flags = [], [], []
        for j in range(len(nodes) // 2):
            flip = order_ref[j * 2 ** (level + 1) + 2**level - 1] == 1
            level_flags.append(flip)
            lower, upper = nodes[2 * j], nodes[2 * j + 1]
            first = [jnp.where(flip, b, a) for a, b in zip(lower, upper)]
            second = [jnp.where(flip, a, b) for a, b in zip(lower, upper)]
            parts = [dot_high(first_mix, a) for a in first] + [dot_high(second_mix, a) for a in second]
            if level == 0:
                parts = [parts[0] + parts[1]]
            merged.append(parts)
            level_products.append(
                {(a, b): total(parts[a] * parts[b]) for a in range(len(parts)) for b in range(a + 1)}
            )
        nodes = merged
        products.append(level_products)
        flags.append(level_flags)
    lane = lax.broadcasted_iota(jnp.int32, (8, LANES), 1)
    packed = jnp.zeros((8, LANES), f32)
    for index, value in enumerate(sums):
        packed = jnp.where(lane == index, value, packed)
    sums_z[z] = packed
    for copy in exchange("tensor", 2, lambda t: sums_z.at[z], sums_z.at[z]):
        copy.wait()
    packed = sums_z[0]
    for index in range(1, n_tp):
        packed = packed + sums_z[index]
    sums_p[me] = packed
    for copy in exchange("dp", 1, lambda t: sums_p.at[me], sums_p.at[me]):
        copy.wait()
    packed = sums_p[0]
    for index in range(1, n_dp):
        packed = packed + sums_p[index]
    packed = packed[0:1]
    lane = lax.broadcasted_iota(jnp.int32, (1, LANES), 1)

    def summed(index):
        return jnp.sum(jnp.where(lane == index, packed, 0.0), axis=1, keepdims=True)

    masses = [summed(index) for index in leaf_mass]
    scales = [[jnp.ones((1, 1), f32)] for _ in range(n_dp)]
    for level in range(levels):
        new_masses, new_scales = [], []
        for j, products_of in enumerate(products[level]):
            flip = flags[level][j]
            lower, upper = scales[2 * j], scales[2 * j + 1]
            if level == 0:
                coefs = [jnp.ones((1, 1), f32)]
            else:
                coefs = [jnp.where(flip, b, a) for a, b in zip(lower, upper)]
                coefs += [jnp.where(flip, a, b) for a, b in zip(lower, upper)]
            square = jnp.zeros((1, 1), f32)
            for (a, b), index in products_of.items():
                term = coefs[a] * (coefs[b] * summed(index))
                square = square + (term if a == b else 2.0 * term)
            mass = masses[2 * j] + masses[2 * j + 1]
            scale = jnp.sqrt(mass / (jnp.maximum(square, 0.0) + 1e-06))
            new_masses.append(mass)
            new_scales.append([scale * c for c in coefs])
        masses, scales = new_masses, new_scales
    chunk = scales[0][0] * nodes[0][0]
    for c, part in zip(scales[0][1:], nodes[0][1:]):
        chunk = chunk + c * part
    root[:, tile_of(me)] = chunk

    gram_part[...] = dot_rows(chunk, chunk)

    def rows_of(owner):
        return pl.ds(pl.multiple_of(owner * block, block), block)

    gram_rs[me] = gram_part[rows_of(me), :]
    gram_copies = exchange("dp", 2, lambda t: gram_part.at[rows_of(t)], gram_rs.at[me])
    root_copies = exchange("dp", 3, lambda t: root.at[:, tile_of(me)], root.at[:, tile_of(me)])
    for copy in gram_copies:
        copy.wait()
    part = gram_rs[0]
    for index in range(1, n_dp):
        part = part + gram_rs[index]
    gram_z[z] = part
    for copy in exchange("tensor", 3, lambda t: gram_z.at[z], gram_z.at[z]):
        copy.wait()
    part = gram_z[0]
    for index in range(1, n_tp):
        part = part + gram_z[index]
    gram[rows_of(me), :] = part
    gram_copies = exchange("dp", 4, lambda t: gram.at[rows_of(me)], gram.at[rows_of(me)])
    for copy in root_copies:
        copy.wait()
    root_write = pltpu.make_async_copy(root, root_out, out_sem.at[0])
    root_write.start()
    for index in range(n_tp):
        value = grads[index]
        for tile in range(n_dp):
            pre[index : index + 1, tile * LANES : (tile + 1) * LANES] = value[tile : tile + 1]
    rhs[z] = dot_rows(pre[...], root[...])
    rhs_copies = exchange("tensor", 4, lambda t: rhs.at[z], rhs.at[z])
    for copy in gram_copies:
        copy.wait()

    system = gram[...]
    eye = lax.broadcasted_iota(jnp.int32, system.shape, 0) == lax.broadcasted_iota(
        jnp.int32, system.shape, 1
    )
    trace = jnp.sum(
        jnp.sum(jnp.where(eye, system, 0.0), axis=0, keepdims=True), axis=1, keepdims=True
    )
    damping = trace / rows
    unit = 1.0 / damping
    system = system * unit + jnp.where(eye, 1.0, 0.0)
    first, steps = newton_plan(rows)
    inverse = None
    for scale in steps:
        if inverse is None:
            inverse = jnp.where(eye, 2.0 * first * scale, 0.0) - (first * first * scale) * system
        else:
            residual = jnp.where(eye, 2.0, 0.0) - dot_high(system, inverse)
            inverse = scale * dot_high(inverse, residual)
    for copy in rhs_copies:
        copy.wait()
    target = rhs[0]
    for index in range(1, n_tp):
        target = target + rhs[index]
    target = target * unit
    solved = dot_rows(target, inverse)
    for _ in range(2):
        solved = solved + dot_rows(target - dot_rows(solved, system), inverse)
    pre[...] = pre[...] - dot_high(solved, root[...])
    pre_write = pltpu.make_async_copy(pre, pre_out, out_sem.at[1])
    pre_write.start()
    pre_write.wait()
    root_write.wait()


def fused_body(
    activations,
    out_grads,
    input_proj,
    grad_proj,
    example_count,
    child_order,
    prior_sketch,
    fold_map,
    merge_mix,
):
    n_dp, n_tp = lax.axis_size("dp"), lax.axis_size("tensor")
    rows, columns = prior_sketch.shape
    slots = activations.shape[0] // SEQ
    f32, bf16 = jnp.float32, jnp.bfloat16
    width, hidden = activations.shape[1], out_grads.shape[1]
    phases = 5
    hbm = pl.BlockSpec(memory_space=pl.ANY)
    vmem = pl.BlockSpec(memory_space=pltpu.VMEM)
    smem = pl.BlockSpec(memory_space=pltpu.SMEM)
    return pl.pallas_call(
        functools.partial(fused_kernel, n_dp, n_tp),
        out_shape=(
            jax.ShapeDtypeStruct((rows, columns), f32),
            jax.ShapeDtypeStruct((slots, columns), f32),
        ),
        in_specs=[hbm, hbm, hbm, hbm, smem, smem, hbm, vmem, vmem],
        out_specs=(hbm, hbm),
        scratch_shapes=[
            pltpu.VMEM((slots, SEQ, width), bf16),
            pltpu.VMEM((slots, SEQ, hidden), bf16),
            pltpu.VMEM(input_proj.shape, bf16),
            pltpu.VMEM(grad_proj.shape, bf16),
            pltpu.VMEM((n_dp, rows, LANES), f32),
            pltpu.VMEM((2 * n_tp, SEQ, LANES), f32),
            pltpu.VMEM((n_tp, SEQ, LANES), f32),
            pltpu.VMEM((RANK, LANES), f32),
            pltpu.VMEM((n_tp, n_dp, LANES), f32),
            pltpu.VMEM((n_dp, n_tp, LANES), f32),
            pltpu.VMEM((n_dp, n_tp, LANES), f32),
            pltpu.VMEM((n_tp, 8, LANES), f32),
            pltpu.VMEM((n_dp, 8, LANES), f32),
            pltpu.VMEM((rows, columns), f32),
            pltpu.VMEM((rows, rows), f32),
            pltpu.VMEM((n_dp, rows // n_dp, rows), f32),
            pltpu.VMEM((n_tp, rows // n_dp, rows), f32),
            pltpu.VMEM((rows, rows), f32),
            pltpu.VMEM((n_tp, slots, rows), f32),
            pltpu.VMEM((slots, columns), f32),
            pltpu.SemaphoreType.DMA((3 + 2 * n_tp,)),
            pltpu.SemaphoreType.DMA((n_dp,)),
            pltpu.SemaphoreType.DMA((n_dp,)),
            pltpu.SemaphoreType.DMA((phases, n_tp)),
            pltpu.SemaphoreType.DMA((phases, n_tp)),
            pltpu.SemaphoreType.DMA((phases, n_dp)),
            pltpu.SemaphoreType.DMA((phases, n_dp)),
            pltpu.SemaphoreType.DMA((2,)),
        ],
        compiler_params=pltpu.CompilerParams(
            collective_id=0, has_side_effects=True, vmem_limit_bytes=56 * 2**20
        ),
    )(
        activations,
        out_grads,
        input_proj,
        grad_proj,
        example_count,
        child_order,
        prior_sketch,
        fold_map,
        merge_mix,
    )


def from_partner(value, axis, stride):
    mask = 2**stride
    pairs = [(source, source ^ mask) for source in range(lax.axis_size(axis))]
    return lax.ppermute(value, axis, pairs)


def body(
    activations,
    out_grads,
    input_proj,
    grad_proj,
    example_count,
    child_order,
    prior_sketch,
    fold_map,
    merge_mix,
):
    tensor_count = lax.axis_size("tensor")
    own_rank = RANK // tensor_count
    example_slots = activations.shape[0] // SEQ
    sketch_rows = prior_sketch.shape[0]
    input_part = jnp.dot(activations, input_proj, preferred_element_type=jnp.float32)
    grad_part = jnp.dot(out_grads, grad_proj, preferred_element_type=jnp.float32)
    input_side, grad_side = lax.psum((input_part, grad_part), "tensor")
    grad_own = lax.dynamic_slice_in_dim(grad_side, lax.axis_index("tensor") * own_rank, own_rank, 1)
    grad_blocks = grad_own.reshape(example_slots, SEQ, own_rank)
    input_blocks = input_side.reshape(example_slots, SEQ, RANK)
    example_grad = jnp.einsum(
        "eta,etb->eab", grad_blocks, input_blocks, precision=lax.Precision.HIGHEST
    )
    example_grad = example_grad.reshape(example_slots, own_rank * RANK) / jnp.sqrt(jnp.float32(SEQ))
    live = jnp.arange(example_slots, dtype=jnp.int32) < example_count[0]
    example_grad = jnp.where(live[:, None], example_grad, jnp.zeros_like(example_grad))
    leaf_node = prior_sketch + jnp.dot(fold_map, example_grad, precision=lax.Precision.HIGHEST)
    leaf_weight = lax.psum(jnp.sum(leaf_node * leaf_node), "tensor")
    mix_first = merge_mix[:, :sketch_rows]
    mix_second = merge_mix[:, sketch_rows:]
    depth_count = lax.axis_size("dp").bit_length() - 1
    rank_index = lax.axis_index("dp")
    sketch_node = leaf_node
    sketch_weight = leaf_weight
    for level_index in range(depth_count):
        sibling_node, sibling_weight = from_partner((sketch_node, sketch_weight), "dp", level_index)
        upper_half = rank_index >> level_index & 1
        block_start = rank_index >> level_index + 1 << level_index + 1
        flip_order = child_order[block_start + (1 << level_index) - 1]
        own_first = upper_half == flip_order
        first = jnp.where(own_first, sketch_node, sibling_node)
        second = jnp.where(own_first, sibling_node, sketch_node)
        first_weight = jnp.where(own_first, sketch_weight, sibling_weight)
        second_weight = jnp.where(own_first, sibling_weight, sketch_weight)
        mixture = jnp.dot(mix_first, first, precision=lax.Precision.HIGHEST) + jnp.dot(
            mix_second, second, precision=lax.Precision.HIGHEST
        )
        mix_total = lax.psum(jnp.sum(mixture * mixture), "tensor")
        sketch_weight = first_weight + second_weight
        sketch_node = mixture * jnp.sqrt(sketch_weight / (mix_total + 1e-06))
    gram_part = jnp.dot(sketch_node, sketch_node.T, precision=lax.Precision.HIGHEST)
    product_part = jnp.dot(sketch_node, example_grad.T, precision=lax.Precision.HIGHEST)
    gram, sketch_grad = lax.psum((gram_part, product_part), "tensor")
    damping = jnp.trace(gram) / sketch_rows
    system = gram + damping * jnp.eye(sketch_rows, dtype=jnp.float32)
    factor = jnp.linalg.cholesky(system)
    solved = jax.scipy.linalg.cho_solve((factor, True), sketch_grad)
    preconditioned = example_grad - jnp.dot(solved.T, sketch_node, precision=lax.Precision.HIGHEST)
    return (sketch_node, preconditioned)


def fits_fused(rows, columns, slots, n_dp, n_tp):
    return (
        columns == n_dp * LANES
        and slots == n_tp
        and 2 * RANK == LANES
        and n_dp == 2 ** (n_dp.bit_length() - 1)
        and n_dp % 8 == 0
        and rows % (8 * n_dp) == 0
    )


def step(*args):
    n_dp, n_tp = lax.axis_size("dp"), lax.axis_size("tensor")
    slots = args[0].shape[0] // SEQ
    rows, columns = args[6].shape
    if fits_fused(rows, columns, slots, n_dp, n_tp):
        return fused_body(*args)
    return body(*args)


def solution(mesh):
    in_specs = (
        P("dp", "tensor"),
        P("dp", "tensor"),
        P("tensor", None),
        P("tensor", None),
        P("dp"),
        P(),
        P("dp", "tensor"),
        P(),
        P(),
    )
    out_specs = (P(None, "tensor"), P("dp", "tensor"))
    return jax.shard_map(step, mesh=mesh, in_specs=in_specs, out_specs=out_specs, check_vma=False)
```

```python
import functools

import jax
import jax.numpy as jnp
from jax import lax
from jax.experimental import pallas as pl
from jax.experimental.pallas import tpu as pltpu
from jax.sharding import PartitionSpec as P

RANK = 64
SEQ = 128
LANES = 128
HIGHEST = lax.Precision.HIGHEST
MESH = pl.DeviceIdType.MESH


def newton_plan(rows):
    low, high = 0.999, (rows + 1) * 1.001
    first = 2.0 / (low + high)
    reach, scales = first * low, []
    while 1.0 - reach > 1e-3:
        grown = reach * (2.0 - reach)
        scale = 2.0 / (1.0 + grown)
        scales.append(scale)
        reach = grown * scale
    return first, scales


def dot_high(left, right):
    return jnp.dot(left, right, precision=HIGHEST, preferred_element_type=jnp.float32)


def dot_flip(left, right):
    return lax.dot_general(left, right, (((1,), (1,)), ((), ())), preferred_element_type=jnp.float32)


def dot_rows(left, right):
    return lax.dot_general(
        left, right, (((1,), (1,)), ((), ())), precision=HIGHEST, preferred_element_type=jnp.float32
    )


def halves(value):
    high = value.astype(jnp.bfloat16)
    return high, (value - high.astype(jnp.float32)).astype(jnp.bfloat16)


def dot_halves(left, right):
    (a, b), (c, d) = left, right
    out = jnp.dot(a, c, preferred_element_type=jnp.float32)
    out = out + jnp.dot(a, d, preferred_element_type=jnp.float32)
    return out + jnp.dot(b, c, preferred_element_type=jnp.float32)


def fused_kernel(
    n_dp,
    n_tp,
    act_hbm,
    out_hbm,
    wi_hbm,
    wo_hbm,
    count_ref,
    order_ref,
    prior_hbm,
    fold_ref,
    mix_ref,
    root_out,
    gram_out,
    rhs_out,
    grads_out,
    act,
    outg,
    wi,
    wo,
    prior,
    zsend,
    zrecv,
    full,
    grads,
    grads_by_tile,
    grads_all,
    sums_z,
    sums_p,
    root,
    gram_part,
    gram_rs,
    gram_z,
    gram,
    load_sem,
    prior_send,
    prior_recv,
    z_send,
    z_recv,
    p_send,
    p_recv,
    out_sem,
):
    f32 = jnp.float32
    me, z = lax.axis_index("dp"), lax.axis_index("tensor")
    rows = gram.shape[0]
    block = rows // n_dp
    part_rows = gram_z.shape[1]
    levels = n_dp.bit_length() - 1

    def dp_of(k):
        return lax.rem(me + k, n_dp)

    def tp_of(k):
        return lax.rem(z + k, n_tp)

    order = sorted(range(1, n_tp), key=lambda k: -min(k, n_tp - k)) + [0]
    loads = []
    for index, (src, dst) in enumerate(((wi_hbm, wi), (wo_hbm, wo))):
        loads.append(pltpu.make_async_copy(src, dst, load_sem.at[index]))
        loads[-1].start()
    chunk_loads = []
    for index, k in enumerate(order):
        e = tp_of(k)
        span = pl.ds(pl.multiple_of(e * SEQ, SEQ), SEQ)
        pair = (
            pltpu.make_async_copy(act_hbm.at[span], act.at[index], load_sem.at[2 + 2 * index]),
            pltpu.make_async_copy(out_hbm.at[span], outg.at[index], load_sem.at[3 + 2 * index]),
        )
        for copy in pair:
            copy.start()
        chunk_loads.append(pair)

    def tile_of(owner):
        return pl.ds(pl.multiple_of(owner * LANES, LANES), LANES)

    own_prior = pltpu.make_async_copy(
        prior_hbm.at[:, tile_of(me)], prior.at[me], load_sem.at[2 + 2 * n_tp]
    )
    own_prior.start()

    barrier = pltpu.get_barrier_semaphore()
    for k in range(1, n_dp):
        pl.semaphore_signal(barrier, inc=1, device_id={"dp": dp_of(k)}, device_id_type=MESH)
    for k in range(1, n_tp):
        pl.semaphore_signal(barrier, inc=1, device_id={"tensor": tp_of(k)}, device_id_type=MESH)
    pl.semaphore_wait(barrier, n_dp + n_tp - 2)

    prior_copies = []
    for k in range(1, n_dp):
        prior_copies.append(
            pltpu.make_async_remote_copy(
                src_ref=prior_hbm.at[:, tile_of(dp_of(k))],
                dst_ref=prior.at[me],
                send_sem=prior_send.at[k],
                recv_sem=prior_recv.at[k],
                device_id={"dp": dp_of(k)},
                device_id_type=MESH,
            )
        )
        prior_copies[-1].start()

    def exchange(axis, phase, source, target):
        size, other = (n_tp, tp_of) if axis == "tensor" else (n_dp, dp_of)
        send, recv = (z_send, z_recv) if axis == "tensor" else (p_send, p_recv)
        copies = []
        for k in range(1, size):
            copies.append(
                pltpu.make_async_remote_copy(
                    src_ref=source(other(k)),
                    dst_ref=target,
                    send_sem=send.at[phase, k],
                    recv_sem=recv.at[phase, k],
                    device_id={axis: other(k)},
                    device_id_type=MESH,
                )
            )
            copies[-1].start()
        return copies

    for copy in loads:
        copy.wait()
    side_copies = []
    for index, k in enumerate(order):
        for copy in chunk_loads[index]:
            copy.wait()
        left = dot_flip(act[index], wi[...])
        right = dot_flip(outg[index], wo[...])
        both = jnp.concatenate([left, right], axis=1)
        if k == 0:
            zrecv[z] = both
        else:
            zsend[index] = both
            copy = pltpu.make_async_remote_copy(
                src_ref=zsend.at[index],
                dst_ref=zrecv.at[z],
                send_sem=z_send.at[0, k],
                recv_sem=z_recv.at[0, k],
                device_id={"tensor": tp_of(k)},
                device_id_type=MESH,
            )
            copy.start()
            side_copies.append(copy)
    for copy in side_copies:
        copy.wait()
    sides = zrecv[0]
    for index in range(1, n_tp):
        sides = sides + zrecv[index]
    lane = lax.broadcasted_iota(jnp.int32, sides.shape, 1)
    doubled = jnp.where(lane < RANK, sides, pltpu.roll(sides, RANK, 1))
    product = dot_high(sides.T, doubled) / jnp.sqrt(f32(SEQ))
    product = jnp.where(z < count_ref[0], product, jnp.zeros_like(product))
    full[...] = product[RANK:]
    even = full[pl.ds(0, RANK // 2, stride=2), :]
    odd = full[pl.ds(1, RANK // 2, stride=2), :]
    lane = lax.broadcasted_iota(jnp.int32, even.shape, 1)
    mine = jnp.where(lane < RANK, even, odd)
    for index in range(n_tp):
        zsend[n_tp + index, 0:n_dp, :] = mine[index * n_dp : (index + 1) * n_dp]
    grads[z] = zsend[n_tp + z, 0:n_dp, :]
    for copy in exchange("tensor", 1, lambda t: zsend.at[n_tp + t, 0:n_dp, :], grads.at[z]):
        copy.wait()
    for index in range(n_tp):
        value = grads[index]
        for tile in range(n_dp):
            grads_by_tile[tile, index : index + 1, :] = value[tile : tile + 1]
    grads_all[me] = grads_by_tile[me]
    grad_copies = exchange("dp", 0, lambda t: grads_by_tile.at[t], grads_all.at[me])
    own_prior.wait()
    for copy in prior_copies:
        copy.wait()
    for copy in grad_copies:
        copy.wait()

    fold = fold_ref[...].T
    sums = []

    def total(value):
        sums.append(jnp.sum(jnp.sum(value, axis=0, keepdims=True), axis=1, keepdims=True))
        return len(sums) - 1

    leaves, leaf_mass = [], []
    for r in range(n_dp):
        leaf = prior[r]
        step = grads_all[r]
        for e in range(n_tp):
            leaf = leaf + fold[:, e : e + 1] * step[e : e + 1, :]
        leaf_mass.append(total(leaf * leaf))
        leaves.append([leaf])
    first_mix, second_mix = mix_ref[:, :rows], mix_ref[:, rows:]
    nodes, products, flags = leaves, [], []
    for level in range(levels):
        merged, level_products, level_flags = [], [], []
        for j in range(len(nodes) // 2):
            flip = order_ref[j * 2 ** (level + 1) + 2**level - 1] == 1
            level_flags.append(flip)
            lower, upper = nodes[2 * j], nodes[2 * j + 1]
            first = [jnp.where(flip, b, a) for a, b in zip(lower, upper)]
            second = [jnp.where(flip, a, b) for a, b in zip(lower, upper)]
            parts = [dot_high(first_mix, a) for a in first] + [dot_high(second_mix, a) for a in second]
            if level == 0:
                parts = [parts[0] + parts[1]]
            merged.append(parts)
            level_products.append(
                {(a, b): total(parts[a] * parts[b]) for a in range(len(parts)) for b in range(a + 1)}
            )
        nodes = merged
        products.append(level_products)
        flags.append(level_flags)
    lane = lax.broadcasted_iota(jnp.int32, (8, LANES), 1)
    packed = jnp.zeros((8, LANES), f32)
    for index, value in enumerate(sums):
        packed = jnp.where(lane == index, value, packed)
    sums_z[z] = packed
    for copy in exchange("tensor", 2, lambda t: sums_z.at[z], sums_z.at[z]):
        copy.wait()
    packed = sums_z[0]
    for index in range(1, n_tp):
        packed = packed + sums_z[index]
    sums_p[me] = packed
    for copy in exchange("dp", 1, lambda t: sums_p.at[me], sums_p.at[me]):
        copy.wait()
    packed = sums_p[0]
    for index in range(1, n_dp):
        packed = packed + sums_p[index]
    packed = packed[0:1]
    lane = lax.broadcasted_iota(jnp.int32, (1, LANES), 1)

    def summed(index):
        return jnp.sum(jnp.where(lane == index, packed, 0.0), axis=1, keepdims=True)

    masses = [summed(index) for index in leaf_mass]
    scales = [[jnp.ones((1, 1), f32)] for _ in range(n_dp)]
    for level in range(levels):
        new_masses, new_scales = [], []
        for j, products_of in enumerate(products[level]):
            flip = flags[level][j]
            lower, upper = scales[2 * j], scales[2 * j + 1]
            if level == 0:
                coefs = [jnp.ones((1, 1), f32)]
            else:
                coefs = [jnp.where(flip, b, a) for a, b in zip(lower, upper)]
                coefs += [jnp.where(flip, a, b) for a, b in zip(lower, upper)]
            square = jnp.zeros((1, 1), f32)
            for (a, b), index in products_of.items():
                term = coefs[a] * (coefs[b] * summed(index))
                square = square + (term if a == b else 2.0 * term)
            mass = masses[2 * j] + masses[2 * j + 1]
            scale = jnp.sqrt(mass / (jnp.maximum(square, 0.0) + 1e-06))
            new_masses.append(mass)
            new_scales.append([scale * c for c in coefs])
        masses, scales = new_masses, new_scales
    chunk = scales[0][0] * nodes[0][0]
    for c, part in zip(scales[0][1:], nodes[0][1:]):
        chunk = chunk + c * part
    root[:, tile_of(me)] = chunk

    square = dot_rows(chunk, chunk)
    every = jnp.concatenate([grads_all[r] for r in range(n_dp)], axis=0)
    targets = dot_rows(every, chunk)
    filler = jnp.zeros((part_rows - block - n_tp, rows), f32)
    for r in range(n_dp):
        gram_part[r, 0:block, :] = square[r * block : (r + 1) * block]
        gram_part[r, block:, :] = jnp.concatenate([targets[r * n_tp : (r + 1) * n_tp], filler], axis=0)
    gram_rs[me] = gram_part[me]
    gram_copies = exchange("dp", 2, lambda t: gram_part.at[t], gram_rs.at[me])
    root_copies = exchange("dp", 3, lambda t: root.at[:, tile_of(me)], root.at[:, tile_of(me)])
    for index in range(n_tp):
        value = grads[index]
        for tile in range(n_dp):
            grads_out[index : index + 1, tile * LANES : (tile + 1) * LANES] = value[tile : tile + 1]
    for copy in gram_copies:
        copy.wait()
    part = gram_rs[0]
    for index in range(1, n_dp):
        part = part + gram_rs[index]
    gram_z[z] = part
    for copy in exchange("tensor", 3, lambda t: gram_z.at[z], gram_z.at[z]):
        copy.wait()
    part = gram_z[0]
    for index in range(1, n_tp):
        part = part + gram_z[index]
    own_rows = pl.ds(pl.multiple_of(me * block, block), block)
    gram[own_rows, :] = part[0:block]
    gram_copies = exchange("dp", 4, lambda t: gram.at[own_rows], gram.at[own_rows])
    rhs_out[...] = part[block : block + n_tp]
    for copy in root_copies:
        copy.wait()
    root_write = pltpu.make_async_copy(root, root_out, out_sem.at[0])
    root_write.start()
    for copy in gram_copies:
        copy.wait()
    gram_out[...] = gram[...]
    root_write.wait()


def solve_kernel(root_hbm, gram_ref, rhs_ref, grads_ref, root_out, pre_out, root, sems):
    read = pltpu.make_async_copy(root_hbm, root, sems.at[0])
    read.start()
    system = gram_ref[...]
    rows = system.shape[0]
    eye = lax.broadcasted_iota(jnp.int32, system.shape, 0) == lax.broadcasted_iota(
        jnp.int32, system.shape, 1
    )
    trace = jnp.sum(
        jnp.sum(jnp.where(eye, system, 0.0), axis=0, keepdims=True), axis=1, keepdims=True
    )
    unit = 1.0 / (trace / rows)
    system = system * unit + jnp.where(eye, 1.0, 0.0)
    system_halves = halves(system)
    first, steps = newton_plan(rows)
    inverse = jnp.where(eye, 2.0 * first * steps[0], 0.0) - (first * first * steps[0]) * system
    for scale in steps[1:]:
        inverse_halves = halves(inverse)
        residual = jnp.where(eye, 2.0, 0.0) - dot_halves(system_halves, inverse_halves)
        inverse = scale * dot_halves(inverse_halves, halves(residual))
    read.wait()
    write = pltpu.make_async_copy(root, root_out, sems.at[1])
    write.start()
    target = rhs_ref[...] * unit
    solved = dot_rows(target, inverse)
    for _ in range(2):
        solved = solved + dot_rows(target - dot_rows(solved, system), inverse)
    pre_out[...] = grads_ref[...] - dot_high(solved, root[...])
    write.wait()


def fused_body(
    activations,
    out_grads,
    input_proj,
    grad_proj,
    example_count,
    child_order,
    prior_sketch,
    fold_map,
    merge_mix,
):
    n_dp, n_tp = lax.axis_size("dp"), lax.axis_size("tensor")
    rows, columns = prior_sketch.shape
    slots = activations.shape[0] // SEQ
    f32, bf16 = jnp.float32, jnp.bfloat16
    width, hidden = activations.shape[1], out_grads.shape[1]
    phases = 5
    hbm = pl.BlockSpec(memory_space=pl.ANY)
    vmem = pl.BlockSpec(memory_space=pltpu.VMEM)
    smem = pl.BlockSpec(memory_space=pltpu.SMEM)
    part_rows = -(-(rows // n_dp + slots) // 8) * 8
    root, gram, rhs, grads = pl.pallas_call(
        functools.partial(fused_kernel, n_dp, n_tp),
        out_shape=(
            jax.ShapeDtypeStruct((rows, columns), f32),
            jax.ShapeDtypeStruct((rows, rows), f32),
            jax.ShapeDtypeStruct((slots, rows), f32),
            jax.ShapeDtypeStruct((slots, columns), f32),
        ),
        in_specs=[hbm, hbm, hbm, hbm, smem, smem, hbm, vmem, vmem],
        out_specs=(hbm, vmem, vmem, vmem),
        scratch_shapes=[
            pltpu.VMEM((slots, SEQ, width), bf16),
            pltpu.VMEM((slots, SEQ, hidden), bf16),
            pltpu.VMEM((RANK, width), bf16),
            pltpu.VMEM((RANK, hidden), bf16),
            pltpu.VMEM((n_dp, rows, LANES), f32),
            pltpu.VMEM((2 * n_tp, SEQ, LANES), f32),
            pltpu.VMEM((n_tp, SEQ, LANES), f32),
            pltpu.VMEM((RANK, LANES), f32),
            pltpu.VMEM((n_tp, n_dp, LANES), f32),
            pltpu.VMEM((n_dp, n_tp, LANES), f32),
            pltpu.VMEM((n_dp, n_tp, LANES), f32),
            pltpu.VMEM((n_tp, 8, LANES), f32),
            pltpu.VMEM((n_dp, 8, LANES), f32),
            pltpu.VMEM((rows, columns), f32),
            pltpu.VMEM((n_dp, part_rows, rows), f32),
            pltpu.VMEM((n_dp, part_rows, rows), f32),
            pltpu.VMEM((n_tp, part_rows, rows), f32),
            pltpu.VMEM((rows, rows), f32),
            pltpu.SemaphoreType.DMA((3 + 2 * n_tp,)),
            pltpu.SemaphoreType.DMA((n_dp,)),
            pltpu.SemaphoreType.DMA((n_dp,)),
            pltpu.SemaphoreType.DMA((phases, n_tp)),
            pltpu.SemaphoreType.DMA((phases, n_tp)),
            pltpu.SemaphoreType.DMA((phases, n_dp)),
            pltpu.SemaphoreType.DMA((phases, n_dp)),
            pltpu.SemaphoreType.DMA((1,)),
        ],
        compiler_params=pltpu.CompilerParams(
            collective_id=0, has_side_effects=True, vmem_limit_bytes=56 * 2**20
        ),
    )(
        activations,
        out_grads,
        input_proj.T,
        grad_proj.T,
        example_count,
        child_order,
        prior_sketch,
        fold_map.T,
        merge_mix,
    )
    return pl.pallas_call(
        solve_kernel,
        out_shape=(
            jax.ShapeDtypeStruct((rows, columns), f32),
            jax.ShapeDtypeStruct((slots, columns), f32),
        ),
        in_specs=[hbm, vmem, vmem, vmem],
        out_specs=(hbm, vmem),
        scratch_shapes=[pltpu.VMEM((rows, columns), f32), pltpu.SemaphoreType.DMA((2,))],
        compiler_params=pltpu.CompilerParams(vmem_limit_bytes=56 * 2**20),
    )(root, gram, rhs, grads)


def from_partner(value, axis, stride):
    mask = 2**stride
    pairs = [(source, source ^ mask) for source in range(lax.axis_size(axis))]
    return lax.ppermute(value, axis, pairs)


def body(
    activations,
    out_grads,
    input_proj,
    grad_proj,
    example_count,
    child_order,
    prior_sketch,
    fold_map,
    merge_mix,
):
    tensor_count = lax.axis_size("tensor")
    own_rank = RANK // tensor_count
    example_slots = activations.shape[0] // SEQ
    sketch_rows = prior_sketch.shape[0]
    input_part = jnp.dot(activations, input_proj, preferred_element_type=jnp.float32)
    grad_part = jnp.dot(out_grads, grad_proj, preferred_element_type=jnp.float32)
    input_side, grad_side = lax.psum((input_part, grad_part), "tensor")
    grad_own = lax.dynamic_slice_in_dim(grad_side, lax.axis_index("tensor") * own_rank, own_rank, 1)
    grad_blocks = grad_own.reshape(example_slots, SEQ, own_rank)
    input_blocks = input_side.reshape(example_slots, SEQ, RANK)
    example_grad = jnp.einsum(
        "eta,etb->eab", grad_blocks, input_blocks, precision=lax.Precision.HIGHEST
    )
    example_grad = example_grad.reshape(example_slots, own_rank * RANK) / jnp.sqrt(jnp.float32(SEQ))
    live = jnp.arange(example_slots, dtype=jnp.int32) < example_count[0]
    example_grad = jnp.where(live[:, None], example_grad, jnp.zeros_like(example_grad))
    leaf_node = prior_sketch + jnp.dot(fold_map, example_grad, precision=lax.Precision.HIGHEST)
    leaf_weight = lax.psum(jnp.sum(leaf_node * leaf_node), "tensor")
    mix_first = merge_mix[:, :sketch_rows]
    mix_second = merge_mix[:, sketch_rows:]
    depth_count = lax.axis_size("dp").bit_length() - 1
    rank_index = lax.axis_index("dp")
    sketch_node = leaf_node
    sketch_weight = leaf_weight
    for level_index in range(depth_count):
        sibling_node, sibling_weight = from_partner((sketch_node, sketch_weight), "dp", level_index)
        upper_half = rank_index >> level_index & 1
        block_start = rank_index >> level_index + 1 << level_index + 1
        flip_order = child_order[block_start + (1 << level_index) - 1]
        own_first = upper_half == flip_order
        first = jnp.where(own_first, sketch_node, sibling_node)
        second = jnp.where(own_first, sibling_node, sketch_node)
        first_weight = jnp.where(own_first, sketch_weight, sibling_weight)
        second_weight = jnp.where(own_first, sibling_weight, sketch_weight)
        mixture = jnp.dot(mix_first, first, precision=lax.Precision.HIGHEST) + jnp.dot(
            mix_second, second, precision=lax.Precision.HIGHEST
        )
        mix_total = lax.psum(jnp.sum(mixture * mixture), "tensor")
        sketch_weight = first_weight + second_weight
        sketch_node = mixture * jnp.sqrt(sketch_weight / (mix_total + 1e-06))
    gram_part = jnp.dot(sketch_node, sketch_node.T, precision=lax.Precision.HIGHEST)
    product_part = jnp.dot(sketch_node, example_grad.T, precision=lax.Precision.HIGHEST)
    gram, sketch_grad = lax.psum((gram_part, product_part), "tensor")
    damping = jnp.trace(gram) / sketch_rows
    system = gram + damping * jnp.eye(sketch_rows, dtype=jnp.float32)
    factor = jnp.linalg.cholesky(system)
    solved = jax.scipy.linalg.cho_solve((factor, True), sketch_grad)
    preconditioned = example_grad - jnp.dot(solved.T, sketch_node, precision=lax.Precision.HIGHEST)
    return (sketch_node, preconditioned)


def fits_fused(rows, columns, slots, n_dp, n_tp):
    return (
        columns == n_dp * LANES
        and slots == n_tp
        and 2 * RANK == LANES
        and n_dp == 2 ** (n_dp.bit_length() - 1)
        and n_dp % 8 == 0
        and rows % (8 * n_dp) == 0
    )


def step(*args):
    n_dp, n_tp = lax.axis_size("dp"), lax.axis_size("tensor")
    slots = args[0].shape[0] // SEQ
    rows, columns = args[6].shape
    if fits_fused(rows, columns, slots, n_dp, n_tp):
        return fused_body(*args)
    return body(*args)


def solution(mesh):
    in_specs = (
        P("dp", "tensor"),
        P("dp", "tensor"),
        P("tensor", None),
        P("tensor", None),
        P("dp"),
        P(),
        P("dp", "tensor"),
        P(),
        P(),
    )
    out_specs = (P(None, "tensor"), P("dp", "tensor"))
    return jax.shard_map(step, mesh=mesh, in_specs=in_specs, out_specs=out_specs, check_vma=False)
```

```python
import functools

import jax
import jax.numpy as jnp
from jax import lax
from jax.experimental import pallas as pl
from jax.experimental.pallas import tpu as pltpu
from jax.sharding import PartitionSpec as P

RANK = 64
SEQ = 128
LANES = 128
HIGHEST = lax.Precision.HIGHEST
MESH = pl.DeviceIdType.MESH


def newton_plan(rows):
    low, high = 0.999, (rows + 1) * 1.001
    first = 2.0 / (low + high)
    reach, scales = first * low, []
    while 1.0 - reach > 1e-3:
        grown = reach * (2.0 - reach)
        scale = 2.0 / (1.0 + grown)
        scales.append(scale)
        reach = grown * scale
    return first, scales


def dot_high(left, right):
    return jnp.dot(left, right, precision=HIGHEST, preferred_element_type=jnp.float32)


def dot_flip(left, right):
    return lax.dot_general(left, right, (((1,), (1,)), ((), ())), preferred_element_type=jnp.float32)


def dot_rows(left, right):
    return lax.dot_general(
        left, right, (((1,), (1,)), ((), ())), precision=HIGHEST, preferred_element_type=jnp.float32
    )


def halves(value):
    high = value.astype(jnp.bfloat16)
    return high, (value - high.astype(jnp.float32)).astype(jnp.bfloat16)


def dot_halves(left, right):
    (a, b), (c, d) = left, right
    out = jnp.dot(a, c, preferred_element_type=jnp.float32)
    out = out + jnp.dot(a, d, preferred_element_type=jnp.float32)
    return out + jnp.dot(b, c, preferred_element_type=jnp.float32)


def fused_kernel(
    n_dp,
    n_tp,
    act_hbm,
    out_hbm,
    wi_hbm,
    wo_hbm,
    count_ref,
    order_ref,
    prior_hbm,
    fold_ref,
    mix_ref,
    root_out,
    gram_out,
    rhs_out,
    grads_out,
    act,
    outg,
    wi,
    wo,
    prior,
    pair_in,
    node_send,
    node_recv,
    zsend,
    zrecv,
    full,
    grads,
    grads_by_tile,
    grads_all,
    sums_z,
    sums_p,
    root,
    gram_part,
    gram_rs,
    gram_z,
    gram,
    load_sem,
    pair_sems,
    node_sems,
    root_sems,
    z_send,
    z_recv,
    p_send,
    p_recv,
    out_sem,
):
    f32 = jnp.float32
    me, z = lax.axis_index("dp"), lax.axis_index("tensor")
    rows = gram.shape[0]
    block = rows // n_dp
    part_rows = gram_z.shape[1]
    levels = n_dp.bit_length() - 1

    def dp_of(k):
        return lax.rem(me + k, n_dp)

    def tp_of(k):
        return lax.rem(z + k, n_tp)

    order = sorted(range(1, n_tp), key=lambda k: -min(k, n_tp - k)) + [0]
    loads = []
    for index, (src, dst) in enumerate(((wi_hbm, wi), (wo_hbm, wo))):
        loads.append(pltpu.make_async_copy(src, dst, load_sem.at[index]))
        loads[-1].start()
    chunk_loads = []
    for index, k in enumerate(order):
        e = tp_of(k)
        span = pl.ds(pl.multiple_of(e * SEQ, SEQ), SEQ)
        pair = (
            pltpu.make_async_copy(act_hbm.at[span], act.at[index], load_sem.at[2 + 2 * index]),
            pltpu.make_async_copy(out_hbm.at[span], outg.at[index], load_sem.at[3 + 2 * index]),
        )
        for copy in pair:
            copy.start()
        chunk_loads.append(pair)

    def tile_of(owner):
        return pl.ds(pl.multiple_of(owner * LANES, LANES), LANES)

    own_prior = pltpu.make_async_copy(prior_hbm, prior, load_sem.at[2 + 2 * n_tp])
    own_prior.start()

    barrier = pltpu.get_barrier_semaphore()
    for k in range(1, n_dp):
        pl.semaphore_signal(barrier, inc=1, device_id={"dp": dp_of(k)}, device_id_type=MESH)
    for k in range(1, n_tp):
        pl.semaphore_signal(barrier, inc=1, device_id={"tensor": tp_of(k)}, device_id_type=MESH)
    pl.semaphore_wait(barrier, n_dp + n_tp - 2)

    half = n_dp // 2
    core, chip = lax.rem(me, 2), me // 2
    partner = me + 1 - 2 * core
    chip_x = chip + 1 - 2 * lax.rem(chip, 2)
    chip_y = chip + 2 - 4 * (chip // 2)
    chip_d = half - 1 - chip

    def push(source, target, device, sems, index):
        copy = pltpu.make_async_remote_copy(
            src_ref=source,
            dst_ref=target,
            send_sem=sems.at[0, index],
            recv_sem=sems.at[1, index],
            device_id={"dp": device},
            device_id_type=MESH,
        )
        copy.start()
        return copy

    pair_copies = [
        push(prior_hbm.at[:, tile_of(2 * q + 1 - core)], pair_in.at[q], partner, pair_sems, q)
        for q in range(half)
    ]

    def exchange(axis, phase, source, target):
        size, other = (n_tp, tp_of) if axis == "tensor" else (n_dp, dp_of)
        send, recv = (z_send, z_recv) if axis == "tensor" else (p_send, p_recv)
        copies = []
        for k in range(1, size):
            copies.append(
                pltpu.make_async_remote_copy(
                    src_ref=source(other(k)),
                    dst_ref=target,
                    send_sem=send.at[phase, k],
                    recv_sem=recv.at[phase, k],
                    device_id={axis: other(k)},
                    device_id_type=MESH,
                )
            )
            copies[-1].start()
        return copies

    for copy in loads:
        copy.wait()
    side_copies = []
    for index, k in enumerate(order):
        for copy in chunk_loads[index]:
            copy.wait()
        left = dot_flip(act[index], wi[...])
        right = dot_flip(outg[index], wo[...])
        both = jnp.concatenate([left, right], axis=1)
        if k == 0:
            zrecv[z] = both
        else:
            zsend[index] = both
            copy = pltpu.make_async_remote_copy(
                src_ref=zsend.at[index],
                dst_ref=zrecv.at[z],
                send_sem=z_send.at[0, k],
                recv_sem=z_recv.at[0, k],
                device_id={"tensor": tp_of(k)},
                device_id_type=MESH,
            )
            copy.start()
            side_copies.append(copy)

    first_mix, second_mix = mix_ref[:, :rows], mix_ref[:, rows:]
    own_prior.wait()
    for copy in pair_copies:
        copy.wait()
    own_first = order_ref[2 * chip] == core
    own_half = [prior[:, tile_of(2 * q + core)] for q in range(half)]
    firsts = [jnp.where(own_first, own_half[q], pair_in[q]) for q in range(half)]
    seconds = [jnp.where(own_first, pair_in[q], own_half[q]) for q in range(half)]
    mixed = dot_high(first_mix, jnp.concatenate(firsts, axis=1))
    mixed = mixed + dot_high(second_mix, jnp.concatenate(seconds, axis=1))
    for q in range(half):
        node_send[q] = mixed[:, q * LANES : (q + 1) * LANES]
    node_copies = [
        push(node_send.at[other], node_recv.at[chip], 2 * other + core, node_sems, index)
        for index, other in enumerate((chip_x, chip_y, chip_d))
    ]
    node_recv[chip] = node_send[chip]
    for copy in side_copies:
        copy.wait()
    sides = zrecv[0]
    for index in range(1, n_tp):
        sides = sides + zrecv[index]
    lane = lax.broadcasted_iota(jnp.int32, sides.shape, 1)
    doubled = jnp.where(lane < RANK, sides, pltpu.roll(sides, RANK, 1))
    product = dot_high(sides.T, doubled) / jnp.sqrt(f32(SEQ))
    product = jnp.where(z < count_ref[0], product, jnp.zeros_like(product))
    full[...] = product[RANK:]
    even = full[pl.ds(0, RANK // 2, stride=2), :]
    odd = full[pl.ds(1, RANK // 2, stride=2), :]
    lane = lax.broadcasted_iota(jnp.int32, even.shape, 1)
    mine = jnp.where(lane < RANK, even, odd)
    for index in range(n_tp):
        zsend[n_tp + index, 0:n_dp, :] = mine[index * n_dp : (index + 1) * n_dp]
    grads[z] = zsend[n_tp + z, 0:n_dp, :]
    grad_copies = exchange("tensor", 1, lambda t: zsend.at[n_tp + t, 0:n_dp, :], grads.at[z])

    for copy in node_copies:
        copy.wait()
    flags = [
        [order_ref[j * 2 ** (level + 1) + 2**level - 1] == 1 for j in range(n_dp >> (level + 1))]
        for level in range(levels)
    ]

    def pick(flip, lower, upper):
        first = [jnp.where(flip, b, a) for a, b in zip(lower, upper)]
        return first, [jnp.where(flip, a, b) for a, b in zip(lower, upper)]

    fold_rows = fold_ref[...]
    paths = [[jnp.concatenate([dot_rows(fold_rows, first_mix), dot_rows(fold_rows, second_mix)], axis=0)]]
    for level in range(1, levels):
        paths.append(
            [dot_rows(p, first_mix) for p in paths[-1]] + [dot_rows(p, second_mix) for p in paths[-1]]
        )
    paths = [[p.T for p in level_paths] for level_paths in paths]
    mixtures = [[[node_recv[j]] for j in range(half)]]
    for level in range(1, levels):
        below = mixtures[-1]
        sides_of = [pick(flags[level][j], below[2 * j], below[2 * j + 1]) for j in range(len(below) // 2)]
        count = len(below[0])
        left = dot_high(first_mix, jnp.concatenate([v for first, _ in sides_of for v in first], axis=1))
        right = dot_high(second_mix, jnp.concatenate([v for _, second in sides_of for v in second], axis=1))
        mixtures.append(
            [
                [
                    side[:, (j * count + i) * LANES : (j * count + i + 1) * LANES]
                    for side in (left, right)
                    for i in range(count)
                ]
                for j in range(len(sides_of))
            ]
        )
    for copy in grad_copies:
        copy.wait()
    for index in range(n_tp):
        value = grads[index]
        for tile in range(n_dp):
            grads_by_tile[tile, index : index + 1, :] = value[tile : tile + 1]
    grads_all[me] = grads_by_tile[me]
    grad_copies = exchange("dp", 0, lambda t: grads_by_tile.at[t], grads_all.at[me])
    fold = fold_rows.T
    leaf_square = jnp.zeros((rows, LANES), f32)
    for tile in range(n_dp):
        leaf = prior[:, tile * LANES : (tile + 1) * LANES]
        step = grads_by_tile[tile]
        for e in range(n_tp):
            leaf = leaf + fold[:, e : e + 1] * step[e : e + 1, :]
        leaf_square = leaf_square + leaf * leaf

    def total(value):
        return jnp.sum(jnp.sum(value, axis=0, keepdims=True), axis=1, keepdims=True)

    own_mass = total(leaf_square)
    for copy in grad_copies:
        copy.wait()

    sums, products, nodes = [], [], []
    steps_of = [[grads_all[r]] for r in range(n_dp)]
    for level in range(levels):
        level_products, level_nodes, merged_steps = [], [], []
        for j in range(len(steps_of) // 2):
            first, second = pick(flags[level][j], steps_of[2 * j], steps_of[2 * j + 1])
            if level == 0:
                merged_steps.append([jnp.concatenate([first[0], second[0]], axis=0)])
            else:
                merged_steps.append(first + second)
            parts = [
                v + dot_high(p, g) for v, p, g in zip(mixtures[level][j], paths[level], merged_steps[-1])
            ]
            index_of = {}
            for a in range(len(parts)):
                for b in range(a + 1):
                    index_of[a, b] = n_dp + len(sums)
                    sums.append(total(parts[a] * parts[b]))
            level_products.append(index_of)
            level_nodes.append(parts)
        steps_of = merged_steps
        products.append(level_products)
        nodes = level_nodes
    lane = lax.broadcasted_iota(jnp.int32, (8, LANES), 1)
    packed = jnp.where(lane == me, own_mass, jnp.zeros((8, LANES), f32))
    for index, value in enumerate(sums):
        packed = jnp.where(lane == n_dp + index, value, packed)
    sums_z[z] = packed
    for copy in exchange("tensor", 2, lambda t: sums_z.at[z], sums_z.at[z]):
        copy.wait()
    packed = sums_z[0]
    for index in range(1, n_tp):
        packed = packed + sums_z[index]
    sums_p[me] = packed
    for copy in exchange("dp", 1, lambda t: sums_p.at[me], sums_p.at[me]):
        copy.wait()
    packed = sums_p[0]
    for index in range(1, n_dp):
        packed = packed + sums_p[index]
    packed = packed[0:1]
    lane = lax.broadcasted_iota(jnp.int32, (1, LANES), 1)

    def summed(index):
        return jnp.sum(jnp.where(lane == index, packed, 0.0), axis=1, keepdims=True)

    masses = [summed(index) for index in range(n_dp)]
    scales = [[jnp.ones((1, 1), f32)] for _ in range(n_dp)]
    for level in range(levels):
        new_masses, new_scales = [], []
        for j, products_of in enumerate(products[level]):
            flip = flags[level][j]
            lower, upper = scales[2 * j], scales[2 * j + 1]
            if level == 0:
                coefs = [jnp.ones((1, 1), f32)]
            else:
                coefs = [jnp.where(flip, b, a) for a, b in zip(lower, upper)]
                coefs += [jnp.where(flip, a, b) for a, b in zip(lower, upper)]
            square = jnp.zeros((1, 1), f32)
            for (a, b), index in products_of.items():
                term = coefs[a] * (coefs[b] * summed(index))
                square = square + (term if a == b else 2.0 * term)
            mass = masses[2 * j] + masses[2 * j + 1]
            scale = jnp.sqrt(mass / (jnp.maximum(square, 0.0) + 1e-06))
            new_masses.append(mass)
            new_scales.append([scale * c for c in coefs])
        masses, scales = new_masses, new_scales
    chunk = scales[0][0] * nodes[0][0]
    for c, part in zip(scales[0][1:], nodes[0][1:]):
        chunk = chunk + c * part
    root[:, tile_of(me)] = chunk

    square = dot_rows(chunk, chunk)
    every = jnp.concatenate([grads_all[r] for r in range(n_dp)], axis=0)
    targets = dot_rows(every, chunk)
    filler = jnp.zeros((part_rows - block - n_tp, rows), f32)
    for r in range(n_dp):
        gram_part[r, 0:block, :] = square[r * block : (r + 1) * block]
        gram_part[r, block:, :] = jnp.concatenate([targets[r * n_tp : (r + 1) * n_tp], filler], axis=0)
    gram_rs[me] = gram_part[me]
    gram_copies = exchange("dp", 2, lambda t: gram_part.at[t], gram_rs.at[me])
    dev_x, dev_y, dev_d = (2 * other + core for other in (chip_x, chip_y, chip_d))
    upper, lower = pl.ds(0, rows // 2), pl.ds(rows // 2, rows // 2)

    def relay(index, owner, device, span=slice(None)):
        block_of = root.at[span, tile_of(owner)]
        return push(block_of, block_of, device, root_sems, index)

    relays = [relay(0, me, dev_x), relay(1, me, dev_y), relay(2, me, partner)]
    for index in range(n_tp):
        value = grads[index]
        for tile in range(n_dp):
            grads_out[index : index + 1, tile * LANES : (tile + 1) * LANES] = value[tile : tile + 1]
    for copy in gram_copies:
        copy.wait()
    part = gram_rs[0]
    for index in range(1, n_dp):
        part = part + gram_rs[index]
    gram_z[z] = part
    z_copies = exchange("tensor", 3, lambda t: gram_z.at[z], gram_z.at[z])
    relays[0].wait_recv()
    relays.append(relay(3, dev_x, dev_y, upper))
    relays.append(relay(4, dev_x, partner))
    relays[1].wait_recv()
    relays.append(relay(5, dev_y, dev_x, lower))
    relays.append(relay(6, dev_y, partner))
    for copy in z_copies:
        copy.wait()
    part = gram_z[0]
    for index in range(1, n_tp):
        part = part + gram_z[index]
    own_rows = pl.ds(pl.multiple_of(me * block, block), block)
    gram[own_rows, :] = part[0:block]
    gram_copies = exchange("dp", 4, lambda t: gram.at[own_rows], gram.at[own_rows])
    rhs_out[...] = part[block : block + n_tp]
    relays[3].wait_recv()
    relays[5].wait_recv()
    relays.append(relay(7, dev_d, partner))
    for index, copy in enumerate(relays):
        copy.wait_send()
        if index not in (0, 1, 3, 5):
            copy.wait_recv()
    root_write = pltpu.make_async_copy(root, root_out, out_sem.at[0])
    root_write.start()
    for copy in gram_copies:
        copy.wait()
    gram_out[...] = gram[...]
    root_write.wait()


def solve_kernel(root_hbm, gram_ref, rhs_ref, grads_ref, root_out, pre_out, root, sems):
    read = pltpu.make_async_copy(root_hbm, root, sems.at[0])
    read.start()
    system = gram_ref[...]
    rows = system.shape[0]
    eye = lax.broadcasted_iota(jnp.int32, system.shape, 0) == lax.broadcasted_iota(
        jnp.int32, system.shape, 1
    )
    trace = jnp.sum(
        jnp.sum(jnp.where(eye, system, 0.0), axis=0, keepdims=True), axis=1, keepdims=True
    )
    unit = 1.0 / (trace / rows)
    system = system * unit + jnp.where(eye, 1.0, 0.0)
    system_halves = halves(system)
    first, steps = newton_plan(rows)
    inverse = jnp.where(eye, 2.0 * first * steps[0], 0.0) - (first * first * steps[0]) * system
    for scale in steps[1:]:
        inverse_halves = halves(inverse)
        residual = jnp.where(eye, 2.0, 0.0) - dot_halves(system_halves, inverse_halves)
        inverse = scale * dot_halves(inverse_halves, halves(residual))
    read.wait()
    write = pltpu.make_async_copy(root, root_out, sems.at[1])
    write.start()
    target = rhs_ref[...] * unit
    solved = dot_rows(target, inverse)
    for _ in range(2):
        solved = solved + dot_rows(target - dot_rows(solved, system), inverse)
    pre_out[...] = grads_ref[...] - dot_high(solved, root[...])
    write.wait()


def fused_body(
    activations,
    out_grads,
    input_proj,
    grad_proj,
    example_count,
    child_order,
    prior_sketch,
    fold_map,
    merge_mix,
):
    n_dp, n_tp = lax.axis_size("dp"), lax.axis_size("tensor")
    rows, columns = prior_sketch.shape
    slots = activations.shape[0] // SEQ
    f32, bf16 = jnp.float32, jnp.bfloat16
    width, hidden = activations.shape[1], out_grads.shape[1]
    phases = 5
    hbm = pl.BlockSpec(memory_space=pl.ANY)
    vmem = pl.BlockSpec(memory_space=pltpu.VMEM)
    smem = pl.BlockSpec(memory_space=pltpu.SMEM)
    part_rows = -(-(rows // n_dp + slots) // 8) * 8
    root, gram, rhs, grads = pl.pallas_call(
        functools.partial(fused_kernel, n_dp, n_tp),
        out_shape=(
            jax.ShapeDtypeStruct((rows, columns), f32),
            jax.ShapeDtypeStruct((rows, rows), f32),
            jax.ShapeDtypeStruct((slots, rows), f32),
            jax.ShapeDtypeStruct((slots, columns), f32),
        ),
        in_specs=[hbm, hbm, hbm, hbm, smem, smem, hbm, vmem, vmem],
        out_specs=(hbm, vmem, vmem, vmem),
        scratch_shapes=[
            pltpu.VMEM((slots, SEQ, width), bf16),
            pltpu.VMEM((slots, SEQ, hidden), bf16),
            pltpu.VMEM((RANK, width), bf16),
            pltpu.VMEM((RANK, hidden), bf16),
            pltpu.VMEM((rows, columns), f32),
            pltpu.VMEM((n_dp // 2, rows, LANES), f32),
            pltpu.VMEM((n_dp // 2, rows, LANES), f32),
            pltpu.VMEM((n_dp // 2, rows, LANES), f32),
            pltpu.VMEM((2 * n_tp, SEQ, LANES), f32),
            pltpu.VMEM((n_tp, SEQ, LANES), f32),
            pltpu.VMEM((RANK, LANES), f32),
            pltpu.VMEM((n_tp, n_dp, LANES), f32),
            pltpu.VMEM((n_dp, n_tp, LANES), f32),
            pltpu.VMEM((n_dp, n_tp, LANES), f32),
            pltpu.VMEM((n_tp, 8, LANES), f32),
            pltpu.VMEM((n_dp, 8, LANES), f32),
            pltpu.VMEM((rows, columns), f32),
            pltpu.VMEM((n_dp, part_rows, rows), f32),
            pltpu.VMEM((n_dp, part_rows, rows), f32),
            pltpu.VMEM((n_tp, part_rows, rows), f32),
            pltpu.VMEM((rows, rows), f32),
            pltpu.SemaphoreType.DMA((3 + 2 * n_tp,)),
            pltpu.SemaphoreType.DMA((2, n_dp // 2)),
            pltpu.SemaphoreType.DMA((2, 3)),
            pltpu.SemaphoreType.DMA((2, 8)),
            pltpu.SemaphoreType.DMA((phases, n_tp)),
            pltpu.SemaphoreType.DMA((phases, n_tp)),
            pltpu.SemaphoreType.DMA((phases, n_dp)),
            pltpu.SemaphoreType.DMA((phases, n_dp)),
            pltpu.SemaphoreType.DMA((1,)),
        ],
        compiler_params=pltpu.CompilerParams(
            collective_id=0, has_side_effects=True, vmem_limit_bytes=56 * 2**20
        ),
    )(
        activations,
        out_grads,
        input_proj.T,
        grad_proj.T,
        example_count,
        child_order,
        prior_sketch,
        fold_map.T,
        merge_mix,
    )
    return pl.pallas_call(
        solve_kernel,
        out_shape=(
            jax.ShapeDtypeStruct((rows, columns), f32),
            jax.ShapeDtypeStruct((slots, columns), f32),
        ),
        in_specs=[hbm, vmem, vmem, vmem],
        out_specs=(hbm, vmem),
        scratch_shapes=[pltpu.VMEM((rows, columns), f32), pltpu.SemaphoreType.DMA((2,))],
        compiler_params=pltpu.CompilerParams(vmem_limit_bytes=56 * 2**20),
    )(root, gram, rhs, grads)


def from_partner(value, axis, stride):
    mask = 2**stride
    pairs = [(source, source ^ mask) for source in range(lax.axis_size(axis))]
    return lax.ppermute(value, axis, pairs)


def body(
    activations,
    out_grads,
    input_proj,
    grad_proj,
    example_count,
    child_order,
    prior_sketch,
    fold_map,
    merge_mix,
):
    tensor_count = lax.axis_size("tensor")
    own_rank = RANK // tensor_count
    example_slots = activations.shape[0] // SEQ
    sketch_rows = prior_sketch.shape[0]
    input_part = jnp.dot(activations, input_proj, preferred_element_type=jnp.float32)
    grad_part = jnp.dot(out_grads, grad_proj, preferred_element_type=jnp.float32)
    input_side, grad_side = lax.psum((input_part, grad_part), "tensor")
    grad_own = lax.dynamic_slice_in_dim(grad_side, lax.axis_index("tensor") * own_rank, own_rank, 1)
    grad_blocks = grad_own.reshape(example_slots, SEQ, own_rank)
    input_blocks = input_side.reshape(example_slots, SEQ, RANK)
    example_grad = jnp.einsum(
        "eta,etb->eab", grad_blocks, input_blocks, precision=lax.Precision.HIGHEST
    )
    example_grad = example_grad.reshape(example_slots, own_rank * RANK) / jnp.sqrt(jnp.float32(SEQ))
    live = jnp.arange(example_slots, dtype=jnp.int32) < example_count[0]
    example_grad = jnp.where(live[:, None], example_grad, jnp.zeros_like(example_grad))
    leaf_node = prior_sketch + jnp.dot(fold_map, example_grad, precision=lax.Precision.HIGHEST)
    leaf_weight = lax.psum(jnp.sum(leaf_node * leaf_node), "tensor")
    mix_first = merge_mix[:, :sketch_rows]
    mix_second = merge_mix[:, sketch_rows:]
    depth_count = lax.axis_size("dp").bit_length() - 1
    rank_index = lax.axis_index("dp")
    sketch_node = leaf_node
    sketch_weight = leaf_weight
    for level_index in range(depth_count):
        sibling_node, sibling_weight = from_partner((sketch_node, sketch_weight), "dp", level_index)
        upper_half = rank_index >> level_index & 1
        block_start = rank_index >> level_index + 1 << level_index + 1
        flip_order = child_order[block_start + (1 << level_index) - 1]
        own_first = upper_half == flip_order
        first = jnp.where(own_first, sketch_node, sibling_node)
        second = jnp.where(own_first, sibling_node, sketch_node)
        first_weight = jnp.where(own_first, sketch_weight, sibling_weight)
        second_weight = jnp.where(own_first, sibling_weight, sketch_weight)
        mixture = jnp.dot(mix_first, first, precision=lax.Precision.HIGHEST) + jnp.dot(
            mix_second, second, precision=lax.Precision.HIGHEST
        )
        mix_total = lax.psum(jnp.sum(mixture * mixture), "tensor")
        sketch_weight = first_weight + second_weight
        sketch_node = mixture * jnp.sqrt(sketch_weight / (mix_total + 1e-06))
    gram_part = jnp.dot(sketch_node, sketch_node.T, precision=lax.Precision.HIGHEST)
    product_part = jnp.dot(sketch_node, example_grad.T, precision=lax.Precision.HIGHEST)
    gram, sketch_grad = lax.psum((gram_part, product_part), "tensor")
    damping = jnp.trace(gram) / sketch_rows
    system = gram + damping * jnp.eye(sketch_rows, dtype=jnp.float32)
    factor = jnp.linalg.cholesky(system)
    solved = jax.scipy.linalg.cho_solve((factor, True), sketch_grad)
    preconditioned = example_grad - jnp.dot(solved.T, sketch_node, precision=lax.Precision.HIGHEST)
    return (sketch_node, preconditioned)


def fits_fused(rows, columns, slots, n_dp, n_tp):
    return (
        columns == n_dp * LANES
        and slots == n_tp
        and 2 * RANK == LANES
        and n_dp == 8
        and rows % (8 * n_dp) == 0
    )


def step(*args):
    n_dp, n_tp = lax.axis_size("dp"), lax.axis_size("tensor")
    slots = args[0].shape[0] // SEQ
    rows, columns = args[6].shape
    if fits_fused(rows, columns, slots, n_dp, n_tp):
        return fused_body(*args)
    return body(*args)


def solution(mesh):
    in_specs = (
        P("dp", "tensor"),
        P("dp", "tensor"),
        P("tensor", None),
        P("tensor", None),
        P("dp"),
        P(),
        P("dp", "tensor"),
        P(),
        P(),
    )
    out_specs = (P(None, "tensor"), P("dp", "tensor"))
    return jax.shard_map(step, mesh=mesh, in_specs=in_specs, out_specs=out_specs, check_vma=False)
```

```python
import functools

import jax
import jax.numpy as jnp
from jax import lax
from jax.experimental import pallas as pl
from jax.experimental.pallas import tpu as pltpu
from jax.sharding import PartitionSpec as P

RANK = 64
SEQ = 128
LANES = 128
HIGHEST = lax.Precision.HIGHEST
MESH = pl.DeviceIdType.MESH


def newton_plan(rows):
    low, high = 0.999, (rows + 1) * 1.001
    first = 2.0 / (low + high)
    reach, scales = first * low, []
    while 1.0 - reach > 1e-3:
        grown = reach * (2.0 - reach)
        scale = 2.0 / (1.0 + grown)
        scales.append(scale)
        reach = grown * scale
    return first, scales


def dot_high(left, right):
    return jnp.dot(left, right, precision=HIGHEST, preferred_element_type=jnp.float32)


def dot_flip(left, right):
    return lax.dot_general(left, right, (((1,), (1,)), ((), ())), preferred_element_type=jnp.float32)


def dot_rows(left, right):
    return lax.dot_general(
        left, right, (((1,), (1,)), ((), ())), precision=HIGHEST, preferred_element_type=jnp.float32
    )


def halves(value):
    high = value.astype(jnp.bfloat16)
    return high, (value - high.astype(jnp.float32)).astype(jnp.bfloat16)


def dot_halves(left, right):
    (a, b), (c, d) = left, right
    out = jnp.dot(a, c, preferred_element_type=jnp.float32)
    out = out + jnp.dot(a, d, preferred_element_type=jnp.float32)
    return out + jnp.dot(b, c, preferred_element_type=jnp.float32)


def dot_mid(left, right):
    return dot_halves(halves(left), halves(right))


def stacked(value, order):
    high = value.astype(jnp.bfloat16).astype(jnp.float32)
    both = (high, value - high)
    return jnp.concatenate([both[i] for i in order], axis=0)


def fused_kernel(
    n_dp,
    n_tp,
    act_hbm,
    out_hbm,
    wi_hbm,
    wo_hbm,
    count_ref,
    order_ref,
    prior_hbm,
    fold_ref,
    mix_ref,
    root_out,
    gram_out,
    rhs_out,
    grads_out,
    act,
    outg,
    wi,
    wo,
    prior,
    pair_in,
    node_send,
    node_recv,
    zsend,
    zrecv,
    full,
    grads,
    grads_by_tile,
    grads_all,
    sums_z,
    sums_p,
    root,
    gram_part,
    gram_rs,
    gram_z,
    gram,
    load_sem,
    pair_sems,
    node_sems,
    root_sems,
    z_send,
    z_recv,
    p_send,
    p_recv,
    out_sem,
):
    f32 = jnp.float32
    me, z = lax.axis_index("dp"), lax.axis_index("tensor")
    rows = gram.shape[0]
    block = rows // n_dp
    part_rows = gram_z.shape[1]
    levels = n_dp.bit_length() - 1

    def dp_of(k):
        return lax.rem(me + k, n_dp)

    def tp_of(k):
        return lax.rem(z + k, n_tp)

    order = sorted(range(1, n_tp), key=lambda k: -min(k, n_tp - k)) + [0]
    loads = []
    for index, (src, dst) in enumerate(((wi_hbm, wi), (wo_hbm, wo))):
        loads.append(pltpu.make_async_copy(src, dst, load_sem.at[index]))
        loads[-1].start()
    chunk_loads = []
    for index, k in enumerate(order):
        e = tp_of(k)
        span = pl.ds(pl.multiple_of(e * SEQ, SEQ), SEQ)
        pair = (
            pltpu.make_async_copy(act_hbm.at[span], act.at[index], load_sem.at[2 + 2 * index]),
            pltpu.make_async_copy(out_hbm.at[span], outg.at[index], load_sem.at[3 + 2 * index]),
        )
        for copy in pair:
            copy.start()
        chunk_loads.append(pair)

    def tile_of(owner):
        return pl.ds(pl.multiple_of(owner * LANES, LANES), LANES)

    own_prior = pltpu.make_async_copy(prior_hbm, prior, load_sem.at[2 + 2 * n_tp])
    own_prior.start()

    barrier = pltpu.get_barrier_semaphore()
    for k in range(1, n_dp):
        pl.semaphore_signal(barrier, inc=1, device_id={"dp": dp_of(k)}, device_id_type=MESH)
    for k in range(1, n_tp):
        pl.semaphore_signal(barrier, inc=1, device_id={"tensor": tp_of(k)}, device_id_type=MESH)
    pl.semaphore_wait(barrier, n_dp + n_tp - 2)

    half = n_dp // 2
    core, chip = lax.rem(me, 2), me // 2
    partner = me + 1 - 2 * core
    chip_x = chip + 1 - 2 * lax.rem(chip, 2)
    chip_y = chip + 2 - 4 * (chip // 2)
    chip_d = half - 1 - chip

    def push(source, target, device, sems, index):
        copy = pltpu.make_async_remote_copy(
            src_ref=source,
            dst_ref=target,
            send_sem=sems.at[0, index],
            recv_sem=sems.at[1, index],
            device_id={"dp": device},
            device_id_type=MESH,
        )
        copy.start()
        return copy

    pair_copies = [
        push(prior_hbm.at[:, tile_of(2 * q + 1 - core)], pair_in.at[q], partner, pair_sems, q)
        for q in range(half)
    ]

    def exchange(axis, phase, source, target):
        size, other = (n_tp, tp_of) if axis == "tensor" else (n_dp, dp_of)
        send, recv = (z_send, z_recv) if axis == "tensor" else (p_send, p_recv)
        copies = []
        for k in range(1, size):
            copies.append(
                pltpu.make_async_remote_copy(
                    src_ref=source(other(k)),
                    dst_ref=target,
                    send_sem=send.at[phase, k],
                    recv_sem=recv.at[phase, k],
                    device_id={axis: other(k)},
                    device_id_type=MESH,
                )
            )
            copies[-1].start()
        return copies

    for copy in loads:
        copy.wait()
    side_copies = []
    for index, k in enumerate(order):
        for copy in chunk_loads[index]:
            copy.wait()
        left = dot_flip(act[index], wi[...])
        right = dot_flip(outg[index], wo[...])
        both = jnp.concatenate([left, right], axis=1)
        if k == 0:
            zrecv[z] = both
        else:
            zsend[index] = both
            copy = pltpu.make_async_remote_copy(
                src_ref=zsend.at[index],
                dst_ref=zrecv.at[z],
                send_sem=z_send.at[0, k],
                recv_sem=z_recv.at[0, k],
                device_id={"tensor": tp_of(k)},
                device_id_type=MESH,
            )
            copy.start()
            side_copies.append(copy)

    first_mix, second_mix = mix_ref[:, :rows], mix_ref[:, rows:]
    own_prior.wait()
    for copy in pair_copies:
        copy.wait()
    own_first = order_ref[2 * chip] == core
    own_half = [prior[:, tile_of(2 * q + core)] for q in range(half)]
    firsts = [jnp.where(own_first, own_half[q], pair_in[q]) for q in range(half)]
    seconds = [jnp.where(own_first, pair_in[q], own_half[q]) for q in range(half)]
    first_halves, second_halves = halves(first_mix), halves(second_mix)
    mixed = dot_halves(first_halves, halves(jnp.concatenate(firsts, axis=1)))
    mixed = mixed + dot_halves(second_halves, halves(jnp.concatenate(seconds, axis=1)))
    for q in range(half):
        node_send[q] = mixed[:, q * LANES : (q + 1) * LANES]
    node_copies = [
        push(node_send.at[other], node_recv.at[chip], 2 * other + core, node_sems, index)
        for index, other in enumerate((chip_x, chip_y, chip_d))
    ]
    node_recv[chip] = node_send[chip]
    for copy in side_copies:
        copy.wait()
    sides = zrecv[0]
    for index in range(1, n_tp):
        sides = sides + zrecv[index]
    lane = lax.broadcasted_iota(jnp.int32, sides.shape, 1)
    doubled = jnp.where(lane < RANK, sides, pltpu.roll(sides, RANK, 1))
    product = dot_mid(sides.T, doubled) / jnp.sqrt(f32(SEQ))
    product = jnp.where(z < count_ref[0], product, jnp.zeros_like(product))
    full[...] = product[RANK:]
    even = full[pl.ds(0, RANK // 2, stride=2), :]
    odd = full[pl.ds(1, RANK // 2, stride=2), :]
    lane = lax.broadcasted_iota(jnp.int32, even.shape, 1)
    mine = jnp.where(lane < RANK, even, odd)
    for index in range(n_tp):
        zsend[n_tp + index, 0:n_dp, :] = mine[index * n_dp : (index + 1) * n_dp]
    grads[z] = zsend[n_tp + z, 0:n_dp, :]
    grad_copies = exchange("tensor", 1, lambda t: zsend.at[n_tp + t, 0:n_dp, :], grads.at[z])

    flags = [
        [order_ref[j * 2 ** (level + 1) + 2**level - 1] == 1 for j in range(n_dp >> (level + 1))]
        for level in range(levels)
    ]

    def pick(flip, lower, upper):
        first = [jnp.where(flip, b, a) for a, b in zip(lower, upper)]
        return first, [jnp.where(flip, a, b) for a, b in zip(lower, upper)]

    fold_rows = fold_ref[...]
    paths = [[jnp.concatenate([dot_rows(fold_rows, first_mix), dot_rows(fold_rows, second_mix)], axis=0)]]
    for level in range(1, levels):
        paths.append(
            [dot_rows(p, first_mix) for p in paths[-1]] + [dot_rows(p, second_mix) for p in paths[-1]]
        )
    paths = [[stacked(p, (0, 0, 1)).T.astype(jnp.bfloat16) for p in level] for level in paths]
    for copy in grad_copies:
        copy.wait()
    for index in range(n_tp):
        value = grads[index]
        for tile in range(n_dp):
            grads_by_tile[tile, index : index + 1, :] = value[tile : tile + 1]
    grads_all[me] = grads_by_tile[me]
    grad_copies = exchange("dp", 0, lambda t: grads_by_tile.at[t], grads_all.at[me])
    fold = fold_rows.T
    leaf_square = jnp.zeros((rows, LANES), f32)
    for tile in range(n_dp):
        leaf = prior[:, tile * LANES : (tile + 1) * LANES]
        step = grads_by_tile[tile]
        for e in range(n_tp):
            leaf = leaf + fold[:, e : e + 1] * step[e : e + 1, :]
        leaf_square = leaf_square + leaf * leaf

    def total(value):
        return jnp.sum(jnp.sum(value, axis=0, keepdims=True), axis=1, keepdims=True)

    own_mass = total(leaf_square)

    for copy in node_copies:
        copy.wait()
    mixtures = [[[node_recv[j]] for j in range(half)]]
    for level in range(1, levels):
        below = mixtures[-1]
        sides_of = [pick(flags[level][j], below[2 * j], below[2 * j + 1]) for j in range(len(below) // 2)]
        count = len(below[0])
        left = dot_halves(first_halves, halves(jnp.concatenate([v for f, _ in sides_of for v in f], axis=1)))
        right = dot_halves(second_halves, halves(jnp.concatenate([v for _, g in sides_of for v in g], axis=1)))
        mixtures.append(
            [
                [
                    side[:, (j * count + i) * LANES : (j * count + i + 1) * LANES]
                    for side in (left, right)
                    for i in range(count)
                ]
                for j in range(len(sides_of))
            ]
        )
    for copy in grad_copies:
        copy.wait()

    sums, products, nodes = [], [], []
    steps_of = [[grads_all[r]] for r in range(n_dp)]
    for level in range(levels):
        level_products, level_nodes, merged_steps = [], [], []
        for j in range(len(steps_of) // 2):
            first, second = pick(flags[level][j], steps_of[2 * j], steps_of[2 * j + 1])
            if level == 0:
                merged_steps.append([jnp.concatenate([first[0], second[0]], axis=0)])
            else:
                merged_steps.append(first + second)
        updates = [
            jnp.dot(
                path,
                jnp.concatenate([stacked(g[i], (0, 1, 0)) for g in merged_steps], axis=1).astype(jnp.bfloat16),
                preferred_element_type=f32,
            )
            for i, path in enumerate(paths[level])
        ]
        for j in range(len(merged_steps)):
            parts = [
                v + update[:, j * LANES : (j + 1) * LANES]
                for v, update in zip(mixtures[level][j], updates)
            ]
            index_of = {}
            for a in range(len(parts)):
                for b in range(a + 1):
                    index_of[a, b] = n_dp + len(sums)
                    sums.append(total(parts[a] * parts[b]))
            level_products.append(index_of)
            level_nodes.append(parts)
        steps_of = merged_steps
        products.append(level_products)
        nodes = level_nodes
    lane = lax.broadcasted_iota(jnp.int32, (8, LANES), 1)
    packed = jnp.where(lane == me, own_mass, jnp.zeros((8, LANES), f32))
    for index, value in enumerate(sums):
        packed = jnp.where(lane == n_dp + index, value, packed)
    sums_z[z] = packed
    for copy in exchange("tensor", 2, lambda t: sums_z.at[z], sums_z.at[z]):
        copy.wait()
    packed = sums_z[0]
    for index in range(1, n_tp):
        packed = packed + sums_z[index]
    sums_p[me] = packed
    for copy in exchange("dp", 1, lambda t: sums_p.at[me], sums_p.at[me]):
        copy.wait()
    packed = sums_p[0]
    for index in range(1, n_dp):
        packed = packed + sums_p[index]
    packed = packed[0:1]
    lane = lax.broadcasted_iota(jnp.int32, (1, LANES), 1)

    def summed(index):
        return jnp.sum(jnp.where(lane == index, packed, 0.0), axis=1, keepdims=True)

    masses = [summed(index) for index in range(n_dp)]
    scales = [[jnp.ones((1, 1), f32)] for _ in range(n_dp)]
    for level in range(levels):
        new_masses, new_scales = [], []
        for j, products_of in enumerate(products[level]):
            flip = flags[level][j]
            lower, upper = scales[2 * j], scales[2 * j + 1]
            if level == 0:
                coefs = [jnp.ones((1, 1), f32)]
            else:
                coefs = [jnp.where(flip, b, a) for a, b in zip(lower, upper)]
                coefs += [jnp.where(flip, a, b) for a, b in zip(lower, upper)]
            square = jnp.zeros((1, 1), f32)
            for (a, b), index in products_of.items():
                term = coefs[a] * (coefs[b] * summed(index))
                square = square + (term if a == b else 2.0 * term)
            mass = masses[2 * j] + masses[2 * j + 1]
            scale = jnp.sqrt(mass / (jnp.maximum(square, 0.0) + 1e-06))
            new_masses.append(mass)
            new_scales.append([scale * c for c in coefs])
        masses, scales = new_masses, new_scales
    chunk = scales[0][0] * nodes[0][0]
    for c, part in zip(scales[0][1:], nodes[0][1:]):
        chunk = chunk + c * part
    root[:, tile_of(me)] = chunk

    square_halves = halves(chunk)
    square = dot_flip(square_halves[0], square_halves[0]) + dot_flip(*square_halves)
    square = square + dot_flip(square_halves[1], square_halves[0])
    every = jnp.concatenate([grads_all[r] for r in range(n_dp)], axis=0)
    targets = dot_rows(every, chunk)
    filler = jnp.zeros((part_rows - block - n_tp, rows), f32)
    for r in range(n_dp):
        gram_part[r, 0:block, :] = square[r * block : (r + 1) * block]
        gram_part[r, block:, :] = jnp.concatenate([targets[r * n_tp : (r + 1) * n_tp], filler], axis=0)
    gram_rs[me] = gram_part[me]
    gram_copies = exchange("dp", 2, lambda t: gram_part.at[t], gram_rs.at[me])
    dev_x, dev_y, dev_d = (2 * other + core for other in (chip_x, chip_y, chip_d))
    upper, lower = pl.ds(0, rows // 2), pl.ds(rows // 2, rows // 2)

    def relay(index, owner, device, span=slice(None)):
        block_of = root.at[span, tile_of(owner)]
        return push(block_of, block_of, device, root_sems, index)

    relays = [relay(0, me, dev_x), relay(1, me, dev_y), relay(2, me, partner)]
    for index in range(n_tp):
        value = grads[index]
        for tile in range(n_dp):
            grads_out[index : index + 1, tile * LANES : (tile + 1) * LANES] = value[tile : tile + 1]
    for copy in gram_copies:
        copy.wait()
    part = gram_rs[0]
    for index in range(1, n_dp):
        part = part + gram_rs[index]
    gram_z[z] = part
    z_copies = exchange("tensor", 3, lambda t: gram_z.at[z], gram_z.at[z])
    relays[0].wait_recv()
    relays.append(relay(3, dev_x, dev_y, upper))
    relays.append(relay(4, dev_x, partner))
    relays[1].wait_recv()
    relays.append(relay(5, dev_y, dev_x, lower))
    relays.append(relay(6, dev_y, partner))
    for copy in z_copies:
        copy.wait()
    part = gram_z[0]
    for index in range(1, n_tp):
        part = part + gram_z[index]
    own_rows = pl.ds(pl.multiple_of(me * block, block), block)
    gram[own_rows, :] = part[0:block]
    gram_copies = exchange("dp", 4, lambda t: gram.at[own_rows], gram.at[own_rows])
    rhs_out[...] = part[block : block + n_tp]
    relays[3].wait_recv()
    relays[5].wait_recv()
    relays.append(relay(7, dev_d, partner))
    for index, copy in enumerate(relays):
        copy.wait_send()
        if index not in (0, 1, 3, 5):
            copy.wait_recv()
    root_write = pltpu.make_async_copy(root, root_out, out_sem.at[0])
    root_write.start()
    for copy in gram_copies:
        copy.wait()
    gram_out[...] = gram[...]
    root_write.wait()


def solve_kernel(root_hbm, gram_ref, rhs_ref, grads_ref, root_out, pre_out, root, sems):
    read = pltpu.make_async_copy(root_hbm, root, sems.at[0])
    read.start()
    system = gram_ref[...]
    rows = system.shape[0]
    eye = lax.broadcasted_iota(jnp.int32, system.shape, 0) == lax.broadcasted_iota(
        jnp.int32, system.shape, 1
    )
    trace = jnp.sum(
        jnp.sum(jnp.where(eye, system, 0.0), axis=0, keepdims=True), axis=1, keepdims=True
    )
    unit = 1.0 / (trace / rows)
    system = system * unit + jnp.where(eye, 1.0, 0.0)
    system_halves = halves(system)
    first, steps = newton_plan(rows)
    inverse = jnp.where(eye, 2.0 * first * steps[0], 0.0) - (first * first * steps[0]) * system
    for scale in steps[1:]:
        inverse_halves = halves(inverse)
        residual = jnp.where(eye, 2.0, 0.0) - dot_halves(system_halves, inverse_halves)
        inverse = scale * dot_halves(inverse_halves, halves(residual))
    read.wait()
    write = pltpu.make_async_copy(root, root_out, sems.at[1])
    write.start()
    target = rhs_ref[...] * unit
    solved = dot_rows(target, inverse)
    for _ in range(2):
        solved = solved + dot_rows(target - dot_rows(solved, system), inverse)
    pre_out[...] = grads_ref[...] - dot_high(solved, root[...])
    write.wait()


def fused_body(
    activations,
    out_grads,
    input_proj,
    grad_proj,
    example_count,
    child_order,
    prior_sketch,
    fold_map,
    merge_mix,
):
    n_dp, n_tp = lax.axis_size("dp"), lax.axis_size("tensor")
    rows, columns = prior_sketch.shape
    slots = activations.shape[0] // SEQ
    f32, bf16 = jnp.float32, jnp.bfloat16
    width, hidden = activations.shape[1], out_grads.shape[1]
    phases = 5
    hbm = pl.BlockSpec(memory_space=pl.ANY)
    vmem = pl.BlockSpec(memory_space=pltpu.VMEM)
    smem = pl.BlockSpec(memory_space=pltpu.SMEM)
    part_rows = -(-(rows // n_dp + slots) // 8) * 8
    root, gram, rhs, grads = pl.pallas_call(
        functools.partial(fused_kernel, n_dp, n_tp),
        out_shape=(
            jax.ShapeDtypeStruct((rows, columns), f32),
            jax.ShapeDtypeStruct((rows, rows), f32),
            jax.ShapeDtypeStruct((slots, rows), f32),
            jax.ShapeDtypeStruct((slots, columns), f32),
        ),
        in_specs=[hbm, hbm, hbm, hbm, smem, smem, hbm, vmem, vmem],
        out_specs=(hbm, vmem, vmem, vmem),
        scratch_shapes=[
            pltpu.VMEM((slots, SEQ, width), bf16),
            pltpu.VMEM((slots, SEQ, hidden), bf16),
            pltpu.VMEM((RANK, width), bf16),
            pltpu.VMEM((RANK, hidden), bf16),
            pltpu.VMEM((rows, columns), f32),
            pltpu.VMEM((n_dp // 2, rows, LANES), f32),
            pltpu.VMEM((n_dp // 2, rows, LANES), f32),
            pltpu.VMEM((n_dp // 2, rows, LANES), f32),
            pltpu.VMEM((2 * n_tp, SEQ, LANES), f32),
            pltpu.VMEM((n_tp, SEQ, LANES), f32),
            pltpu.VMEM((RANK, LANES), f32),
            pltpu.VMEM((n_tp, n_dp, LANES), f32),
            pltpu.VMEM((n_dp, n_tp, LANES), f32),
            pltpu.VMEM((n_dp, n_tp, LANES), f32),
            pltpu.VMEM((n_tp, 8, LANES), f32),
            pltpu.VMEM((n_dp, 8, LANES), f32),
            pltpu.VMEM((rows, columns), f32),
            pltpu.VMEM((n_dp, part_rows, rows), f32),
            pltpu.VMEM((n_dp, part_rows, rows), f32),
            pltpu.VMEM((n_tp, part_rows, rows), f32),
            pltpu.VMEM((rows, rows), f32),
            pltpu.SemaphoreType.DMA((3 + 2 * n_tp,)),
            pltpu.SemaphoreType.DMA((2, n_dp // 2)),
            pltpu.SemaphoreType.DMA((2, 3)),
            pltpu.SemaphoreType.DMA((2, 8)),
            pltpu.SemaphoreType.DMA((phases, n_tp)),
            pltpu.SemaphoreType.DMA((phases, n_tp)),
            pltpu.SemaphoreType.DMA((phases, n_dp)),
            pltpu.SemaphoreType.DMA((phases, n_dp)),
            pltpu.SemaphoreType.DMA((1,)),
        ],
        compiler_params=pltpu.CompilerParams(
            collective_id=0, has_side_effects=True, vmem_limit_bytes=56 * 2**20
        ),
    )(
        activations,
        out_grads,
        input_proj.T,
        grad_proj.T,
        example_count,
        child_order,
        prior_sketch,
        fold_map.T,
        merge_mix,
    )
    return pl.pallas_call(
        solve_kernel,
        out_shape=(
            jax.ShapeDtypeStruct((rows, columns), f32),
            jax.ShapeDtypeStruct((slots, columns), f32),
        ),
        in_specs=[hbm, vmem, vmem, vmem],
        out_specs=(hbm, vmem),
        scratch_shapes=[pltpu.VMEM((rows, columns), f32), pltpu.SemaphoreType.DMA((2,))],
        compiler_params=pltpu.CompilerParams(vmem_limit_bytes=56 * 2**20),
    )(root, gram, rhs, grads)


def from_partner(value, axis, stride):
    mask = 2**stride
    pairs = [(source, source ^ mask) for source in range(lax.axis_size(axis))]
    return lax.ppermute(value, axis, pairs)


def body(
    activations,
    out_grads,
    input_proj,
    grad_proj,
    example_count,
    child_order,
    prior_sketch,
    fold_map,
    merge_mix,
):
    tensor_count = lax.axis_size("tensor")
    own_rank = RANK // tensor_count
    example_slots = activations.shape[0] // SEQ
    sketch_rows = prior_sketch.shape[0]
    input_part = jnp.dot(activations, input_proj, preferred_element_type=jnp.float32)
    grad_part = jnp.dot(out_grads, grad_proj, preferred_element_type=jnp.float32)
    input_side, grad_side = lax.psum((input_part, grad_part), "tensor")
    grad_own = lax.dynamic_slice_in_dim(grad_side, lax.axis_index("tensor") * own_rank, own_rank, 1)
    grad_blocks = grad_own.reshape(example_slots, SEQ, own_rank)
    input_blocks = input_side.reshape(example_slots, SEQ, RANK)
    example_grad = jnp.einsum(
        "eta,etb->eab", grad_blocks, input_blocks, precision=lax.Precision.HIGHEST
    )
    example_grad = example_grad.reshape(example_slots, own_rank * RANK) / jnp.sqrt(jnp.float32(SEQ))
    live = jnp.arange(example_slots, dtype=jnp.int32) < example_count[0]
    example_grad = jnp.where(live[:, None], example_grad, jnp.zeros_like(example_grad))
    leaf_node = prior_sketch + jnp.dot(fold_map, example_grad, precision=lax.Precision.HIGHEST)
    leaf_weight = lax.psum(jnp.sum(leaf_node * leaf_node), "tensor")
    mix_first = merge_mix[:, :sketch_rows]
    mix_second = merge_mix[:, sketch_rows:]
    depth_count = lax.axis_size("dp").bit_length() - 1
    rank_index = lax.axis_index("dp")
    sketch_node = leaf_node
    sketch_weight = leaf_weight
    for level_index in range(depth_count):
        sibling_node, sibling_weight = from_partner((sketch_node, sketch_weight), "dp", level_index)
        upper_half = rank_index >> level_index & 1
        block_start = rank_index >> level_index + 1 << level_index + 1
        flip_order = child_order[block_start + (1 << level_index) - 1]
        own_first = upper_half == flip_order
        first = jnp.where(own_first, sketch_node, sibling_node)
        second = jnp.where(own_first, sibling_node, sketch_node)
        first_weight = jnp.where(own_first, sketch_weight, sibling_weight)
        second_weight = jnp.where(own_first, sibling_weight, sketch_weight)
        mixture = jnp.dot(mix_first, first, precision=lax.Precision.HIGHEST) + jnp.dot(
            mix_second, second, precision=lax.Precision.HIGHEST
        )
        mix_total = lax.psum(jnp.sum(mixture * mixture), "tensor")
        sketch_weight = first_weight + second_weight
        sketch_node = mixture * jnp.sqrt(sketch_weight / (mix_total + 1e-06))
    gram_part = jnp.dot(sketch_node, sketch_node.T, precision=lax.Precision.HIGHEST)
    product_part = jnp.dot(sketch_node, example_grad.T, precision=lax.Precision.HIGHEST)
    gram, sketch_grad = lax.psum((gram_part, product_part), "tensor")
    damping = jnp.trace(gram) / sketch_rows
    system = gram + damping * jnp.eye(sketch_rows, dtype=jnp.float32)
    factor = jnp.linalg.cholesky(system)
    solved = jax.scipy.linalg.cho_solve((factor, True), sketch_grad)
    preconditioned = example_grad - jnp.dot(solved.T, sketch_node, precision=lax.Precision.HIGHEST)
    return (sketch_node, preconditioned)


def fits_fused(rows, columns, slots, n_dp, n_tp):
    return (
        columns == n_dp * LANES
        and slots == n_tp
        and 2 * RANK == LANES
        and n_dp == 8
        and rows % (8 * n_dp) == 0
    )


def step(*args):
    n_dp, n_tp = lax.axis_size("dp"), lax.axis_size("tensor")
    slots = args[0].shape[0] // SEQ
    rows, columns = args[6].shape
    if fits_fused(rows, columns, slots, n_dp, n_tp):
        return fused_body(*args)
    return body(*args)


def solution(mesh):
    in_specs = (
        P("dp", "tensor"),
        P("dp", "tensor"),
        P("tensor", None),
        P("tensor", None),
        P("dp"),
        P(),
        P("dp", "tensor"),
        P(),
        P(),
    )
    out_specs = (P(None, "tensor"), P("dp", "tensor"))
    return jax.shard_map(step, mesh=mesh, in_specs=in_specs, out_specs=out_specs, check_vma=False)
```

```python
import functools

import jax
import jax.numpy as jnp
from jax import lax
from jax.experimental import pallas as pl
from jax.experimental.pallas import tpu as pltpu
from jax.sharding import PartitionSpec as P

RANK = 64
SEQ = 128
LANES = 128
HIGHEST = lax.Precision.HIGHEST
MESH = pl.DeviceIdType.MESH


def newton_plan(rows):
    low, high = 0.999, (rows + 1) * 1.001
    first = 2.0 / (low + high)
    reach, scales = first * low, []
    while 1.0 - reach > 1e-3:
        grown = reach * (2.0 - reach)
        scale = 2.0 / (1.0 + grown)
        scales.append(scale)
        reach = grown * scale
    return first, scales


def dot_high(left, right):
    return jnp.dot(left, right, precision=HIGHEST, preferred_element_type=jnp.float32)


def dot_flip(left, right):
    return lax.dot_general(left, right, (((1,), (1,)), ((), ())), preferred_element_type=jnp.float32)


def dot_rows(left, right):
    return lax.dot_general(
        left, right, (((1,), (1,)), ((), ())), precision=HIGHEST, preferred_element_type=jnp.float32
    )


def halves(value):
    high = value.astype(jnp.bfloat16)
    return high, (value - high.astype(jnp.float32)).astype(jnp.bfloat16)


def dot_halves(left, right):
    (a, b), (c, d) = left, right
    out = jnp.dot(a, c, preferred_element_type=jnp.float32)
    out = out + jnp.dot(a, d, preferred_element_type=jnp.float32)
    return out + jnp.dot(b, c, preferred_element_type=jnp.float32)


def dot_mid(left, right):
    return dot_halves(halves(left), halves(right))


def stacked(value, order):
    high = value.astype(jnp.bfloat16).astype(jnp.float32)
    both = (high, value - high)
    return jnp.concatenate([both[i] for i in order], axis=0)


def fused_kernel(
    n_dp,
    n_tp,
    act_hbm,
    out_hbm,
    wi_hbm,
    wo_hbm,
    count_ref,
    order_ref,
    prior_hbm,
    fold_ref,
    mix_ref,
    root_out,
    gram_out,
    rhs_out,
    grads_out,
    act,
    outg,
    wi,
    wo,
    prior,
    pair_in,
    node_send,
    node_recv,
    zsend,
    zrecv,
    full,
    grads,
    grads_by_tile,
    grads_all,
    sums_z,
    sums_p,
    root,
    gram_part,
    gram_rs,
    gram_z,
    gram,
    load_sem,
    pair_sems,
    node_sems,
    root_sems,
    z_send,
    z_recv,
    p_send,
    p_recv,
    out_sem,
):
    f32 = jnp.float32
    me, z = lax.axis_index("dp"), lax.axis_index("tensor")
    rows = gram.shape[0]
    block = rows // n_dp
    part_rows = gram_z.shape[1]
    levels = n_dp.bit_length() - 1

    def dp_of(k):
        return lax.rem(me + k, n_dp)

    def tp_of(k):
        return lax.rem(z + k, n_tp)

    order = sorted(range(1, n_tp), key=lambda k: -min(k, n_tp - k)) + [0]
    loads = []
    for index, (src, dst) in enumerate(((wi_hbm, wi), (wo_hbm, wo))):
        loads.append(pltpu.make_async_copy(src, dst, load_sem.at[index]))
        loads[-1].start()
    chunk_loads = []
    for index, k in enumerate(order):
        e = tp_of(k)
        span = pl.ds(pl.multiple_of(e * SEQ, SEQ), SEQ)
        pair = (
            pltpu.make_async_copy(act_hbm.at[span], act.at[index], load_sem.at[2 + 2 * index]),
            pltpu.make_async_copy(out_hbm.at[span], outg.at[index], load_sem.at[3 + 2 * index]),
        )
        for copy in pair:
            copy.start()
        chunk_loads.append(pair)

    def tile_of(owner):
        return pl.ds(pl.multiple_of(owner * LANES, LANES), LANES)

    own_prior = pltpu.make_async_copy(prior_hbm, prior, load_sem.at[2 + 2 * n_tp])
    own_prior.start()

    barrier = pltpu.get_barrier_semaphore()
    for k in range(1, n_dp):
        pl.semaphore_signal(barrier, inc=1, device_id={"dp": dp_of(k)}, device_id_type=MESH)
    for k in range(1, n_tp):
        pl.semaphore_signal(barrier, inc=1, device_id={"tensor": tp_of(k)}, device_id_type=MESH)
    pl.semaphore_wait(barrier, n_dp + n_tp - 2)

    half = n_dp // 2
    core, chip = lax.rem(me, 2), me // 2
    partner = me + 1 - 2 * core
    chip_x = chip + 1 - 2 * lax.rem(chip, 2)
    chip_y = chip + 2 - 4 * (chip // 2)
    chip_d = half - 1 - chip

    def push(source, target, device, sems, index):
        copy = pltpu.make_async_remote_copy(
            src_ref=source,
            dst_ref=target,
            send_sem=sems.at[0, index],
            recv_sem=sems.at[1, index],
            device_id={"dp": device},
            device_id_type=MESH,
        )
        copy.start()
        return copy

    pair_copies = [
        push(prior_hbm.at[:, tile_of(2 * q + 1 - core)], pair_in.at[q], partner, pair_sems, q)
        for q in range(half)
    ]

    def exchange(axis, phase, source, target):
        size, other = (n_tp, tp_of) if axis == "tensor" else (n_dp, dp_of)
        send, recv = (z_send, z_recv) if axis == "tensor" else (p_send, p_recv)
        copies = []
        for k in range(1, size):
            copies.append(
                pltpu.make_async_remote_copy(
                    src_ref=source(other(k)),
                    dst_ref=target,
                    send_sem=send.at[phase, k],
                    recv_sem=recv.at[phase, k],
                    device_id={axis: other(k)},
                    device_id_type=MESH,
                )
            )
            copies[-1].start()
        return copies

    for copy in loads:
        copy.wait()
    side_copies = []
    for index, k in enumerate(order):
        for copy in chunk_loads[index]:
            copy.wait()
        left = dot_flip(act[index], wi[...])
        right = dot_flip(outg[index], wo[...])
        both = jnp.concatenate([left, right], axis=1)
        if k == 0:
            zrecv[z] = both
        else:
            zsend[index] = both
            copy = pltpu.make_async_remote_copy(
                src_ref=zsend.at[index],
                dst_ref=zrecv.at[z],
                send_sem=z_send.at[0, k],
                recv_sem=z_recv.at[0, k],
                device_id={"tensor": tp_of(k)},
                device_id_type=MESH,
            )
            copy.start()
            side_copies.append(copy)

    first_mix, second_mix = mix_ref[:, :rows], mix_ref[:, rows:]
    own_prior.wait()
    for copy in pair_copies:
        copy.wait()
    own_first = order_ref[2 * chip] == core
    own_half = [prior[:, tile_of(2 * q + core)] for q in range(half)]
    firsts = [jnp.where(own_first, own_half[q], pair_in[q]) for q in range(half)]
    seconds = [jnp.where(own_first, pair_in[q], own_half[q]) for q in range(half)]
    first_halves, second_halves = halves(first_mix), halves(second_mix)
    mixed = dot_halves(first_halves, halves(jnp.concatenate(firsts, axis=1)))
    mixed = mixed + dot_halves(second_halves, halves(jnp.concatenate(seconds, axis=1)))
    for q in range(half):
        node_send[q] = mixed[:, q * LANES : (q + 1) * LANES]
    node_copies = [
        push(node_send.at[other], node_recv.at[chip], 2 * other + core, node_sems, index)
        for index, other in enumerate((chip_x, chip_y, chip_d))
    ]
    node_recv[chip] = node_send[chip]
    for copy in side_copies:
        copy.wait()
    sides = zrecv[0]
    for index in range(1, n_tp):
        sides = sides + zrecv[index]
    lane = lax.broadcasted_iota(jnp.int32, sides.shape, 1)
    doubled = jnp.where(lane < RANK, sides, pltpu.roll(sides, RANK, 1))
    product = dot_mid(sides.T, doubled) / jnp.sqrt(f32(SEQ))
    product = jnp.where(z < count_ref[0], product, jnp.zeros_like(product))
    full[...] = product[RANK:]
    even = full[pl.ds(0, RANK // 2, stride=2), :]
    odd = full[pl.ds(1, RANK // 2, stride=2), :]
    lane = lax.broadcasted_iota(jnp.int32, even.shape, 1)
    mine = jnp.where(lane < RANK, even, odd)
    for index in range(n_tp):
        zsend[n_tp + index, 0:n_dp, :] = mine[index * n_dp : (index + 1) * n_dp]
    grads[z] = zsend[n_tp + z, 0:n_dp, :]
    grad_copies = exchange("tensor", 1, lambda t: zsend.at[n_tp + t, 0:n_dp, :], grads.at[z])

    flags = [
        [order_ref[j * 2 ** (level + 1) + 2**level - 1] == 1 for j in range(n_dp >> (level + 1))]
        for level in range(levels)
    ]

    def pick(flip, lower, upper):
        first = [jnp.where(flip, b, a) for a, b in zip(lower, upper)]
        return first, [jnp.where(flip, a, b) for a, b in zip(lower, upper)]

    fold_rows = fold_ref[...]
    paths = [[jnp.concatenate([dot_rows(fold_rows, first_mix), dot_rows(fold_rows, second_mix)], axis=0)]]
    for level in range(1, levels):
        paths.append(
            [dot_rows(p, first_mix) for p in paths[-1]] + [dot_rows(p, second_mix) for p in paths[-1]]
        )
    paths = [[stacked(p, (0, 0, 1)).T.astype(jnp.bfloat16) for p in level] for level in paths]
    for copy in grad_copies:
        copy.wait()
    for index in range(n_tp):
        value = grads[index]
        for tile in range(n_dp):
            grads_by_tile[tile, index : index + 1, :] = value[tile : tile + 1]
    grads_all[me] = grads_by_tile[me]
    grad_copies = exchange("dp", 0, lambda t: grads_by_tile.at[t], grads_all.at[me])
    fold = fold_rows.T
    leaf_square = jnp.zeros((rows, LANES), f32)
    for tile in range(n_dp):
        leaf = prior[:, tile * LANES : (tile + 1) * LANES]
        step = grads_by_tile[tile]
        for e in range(n_tp):
            leaf = leaf + fold[:, e : e + 1] * step[e : e + 1, :]
        leaf_square = leaf_square + leaf * leaf

    def total(value):
        return jnp.sum(jnp.sum(value, axis=0, keepdims=True), axis=1, keepdims=True)

    own_mass = total(leaf_square)

    for copy in node_copies:
        copy.wait()
    mixtures = [[[node_recv[j]] for j in range(half)]]
    for level in range(1, levels):
        below = mixtures[-1]
        sides_of = [pick(flags[level][j], below[2 * j], below[2 * j + 1]) for j in range(len(below) // 2)]
        count = len(below[0])
        left = dot_halves(first_halves, halves(jnp.concatenate([v for f, _ in sides_of for v in f], axis=1)))
        right = dot_halves(second_halves, halves(jnp.concatenate([v for _, g in sides_of for v in g], axis=1)))
        mixtures.append(
            [
                [
                    side[:, (j * count + i) * LANES : (j * count + i + 1) * LANES]
                    for side in (left, right)
                    for i in range(count)
                ]
                for j in range(len(sides_of))
            ]
        )
    for copy in grad_copies:
        copy.wait()

    sums, products, nodes = [], [], []
    steps_of = [[grads_all[r]] for r in range(n_dp)]
    for level in range(levels):
        level_products, level_nodes, merged_steps = [], [], []
        for j in range(len(steps_of) // 2):
            first, second = pick(flags[level][j], steps_of[2 * j], steps_of[2 * j + 1])
            if level == 0:
                merged_steps.append([jnp.concatenate([first[0], second[0]], axis=0)])
            else:
                merged_steps.append(first + second)
        updates = [
            jnp.dot(
                path,
                jnp.concatenate([stacked(g[i], (0, 1, 0)) for g in merged_steps], axis=1).astype(jnp.bfloat16),
                preferred_element_type=f32,
            )
            for i, path in enumerate(paths[level])
        ]
        for j in range(len(merged_steps)):
            parts = [
                v + update[:, j * LANES : (j + 1) * LANES]
                for v, update in zip(mixtures[level][j], updates)
            ]
            index_of = {}
            for a in range(len(parts)):
                for b in range(a + 1):
                    index_of[a, b] = n_dp + len(sums)
                    sums.append(total(parts[a] * parts[b]))
            level_products.append(index_of)
            level_nodes.append(parts)
        steps_of = merged_steps
        products.append(level_products)
        nodes = level_nodes
    lane = lax.broadcasted_iota(jnp.int32, (8, LANES), 1)
    packed = jnp.where(lane == me, own_mass, jnp.zeros((8, LANES), f32))
    for index, value in enumerate(sums):
        packed = jnp.where(lane == n_dp + index, value, packed)
    sums_z[z] = packed
    for copy in exchange("tensor", 2, lambda t: sums_z.at[z], sums_z.at[z]):
        copy.wait()
    packed = sums_z[0]
    for index in range(1, n_tp):
        packed = packed + sums_z[index]
    sums_p[me] = packed
    for copy in exchange("dp", 1, lambda t: sums_p.at[me], sums_p.at[me]):
        copy.wait()
    packed = sums_p[0]
    for index in range(1, n_dp):
        packed = packed + sums_p[index]
    packed = packed[0:1]
    lane = lax.broadcasted_iota(jnp.int32, (1, LANES), 1)

    def summed(index):
        return jnp.sum(jnp.where(lane == index, packed, 0.0), axis=1, keepdims=True)

    masses = [summed(index) for index in range(n_dp)]
    scales = [[jnp.ones((1, 1), f32)] for _ in range(n_dp)]
    for level in range(levels):
        new_masses, new_scales = [], []
        for j, products_of in enumerate(products[level]):
            flip = flags[level][j]
            lower, upper = scales[2 * j], scales[2 * j + 1]
            if level == 0:
                coefs = [jnp.ones((1, 1), f32)]
            else:
                coefs = [jnp.where(flip, b, a) for a, b in zip(lower, upper)]
                coefs += [jnp.where(flip, a, b) for a, b in zip(lower, upper)]
            square = jnp.zeros((1, 1), f32)
            for (a, b), index in products_of.items():
                term = coefs[a] * (coefs[b] * summed(index))
                square = square + (term if a == b else 2.0 * term)
            mass = masses[2 * j] + masses[2 * j + 1]
            scale = jnp.sqrt(mass / (jnp.maximum(square, 0.0) + 1e-06))
            new_masses.append(mass)
            new_scales.append([scale * c for c in coefs])
        masses, scales = new_masses, new_scales
    chunk = scales[0][0] * nodes[0][0]
    for c, part in zip(scales[0][1:], nodes[0][1:]):
        chunk = chunk + c * part
    root[:, tile_of(me)] = chunk

    square_halves = halves(chunk)
    square = dot_flip(square_halves[0], square_halves[0]) + dot_flip(*square_halves)
    square = square + dot_flip(square_halves[1], square_halves[0])
    every = jnp.concatenate([grads_all[r] for r in range(n_dp)], axis=0)
    every_halves = halves(every)
    targets = dot_flip(every_halves[0], square_halves[0]) + dot_flip(every_halves[0], square_halves[1])
    targets = targets + dot_flip(every_halves[1], square_halves[0])
    filler = jnp.zeros((part_rows - block - n_tp, rows), f32)
    for r in range(n_dp):
        gram_part[r, 0:block, :] = square[r * block : (r + 1) * block]
        gram_part[r, block:, :] = jnp.concatenate([targets[r * n_tp : (r + 1) * n_tp], filler], axis=0)
    gram_rs[me] = gram_part[me]
    gram_copies = exchange("dp", 2, lambda t: gram_part.at[t], gram_rs.at[me])
    dev_x, dev_y, dev_d = (2 * other + core for other in (chip_x, chip_y, chip_d))
    upper, lower = pl.ds(0, rows // 2), pl.ds(rows // 2, rows // 2)

    def relay(index, owner, device, span=slice(None)):
        block_of = root.at[span, tile_of(owner)]
        return push(block_of, block_of, device, root_sems, index)

    relays = [relay(0, me, dev_x), relay(1, me, dev_y), relay(2, me, partner)]
    for index in range(n_tp):
        value = grads[index]
        for tile in range(n_dp):
            grads_out[index : index + 1, tile * LANES : (tile + 1) * LANES] = value[tile : tile + 1]
    for copy in gram_copies:
        copy.wait()
    part = gram_rs[0]
    for index in range(1, n_dp):
        part = part + gram_rs[index]
    gram_z[z] = part
    z_copies = exchange("tensor", 3, lambda t: gram_z.at[z], gram_z.at[z])
    relays[0].wait_recv()
    relays.append(relay(3, dev_x, dev_y, upper))
    relays.append(relay(4, dev_x, partner))
    relays[1].wait_recv()
    relays.append(relay(5, dev_y, dev_x, lower))
    relays.append(relay(6, dev_y, partner))
    for copy in z_copies:
        copy.wait()
    part = gram_z[0]
    for index in range(1, n_tp):
        part = part + gram_z[index]
    own_rows = pl.ds(pl.multiple_of(me * block, block), block)
    gram[own_rows, :] = part[0:block]
    gram_copies = exchange("dp", 4, lambda t: gram.at[own_rows], gram.at[own_rows])
    rhs_out[...] = part[block : block + n_tp]
    relays[3].wait_recv()
    relays[5].wait_recv()
    relays.append(relay(7, dev_d, partner))
    for index, copy in enumerate(relays):
        copy.wait_send()
        if index not in (0, 1, 3, 5):
            copy.wait_recv()
    root_write = pltpu.make_async_copy(root, root_out, out_sem.at[0])
    root_write.start()
    for copy in gram_copies:
        copy.wait()
    gram_out[...] = gram[...]
    root_write.wait()


def solve_kernel(root_hbm, gram_ref, rhs_ref, grads_ref, root_out, pre_out, root, sems):
    read = pltpu.make_async_copy(root_hbm, root, sems.at[0])
    read.start()
    system = gram_ref[...]
    rows = system.shape[0]
    eye = lax.broadcasted_iota(jnp.int32, system.shape, 0) == lax.broadcasted_iota(
        jnp.int32, system.shape, 1
    )
    trace = jnp.sum(
        jnp.sum(jnp.where(eye, system, 0.0), axis=0, keepdims=True), axis=1, keepdims=True
    )
    unit = 1.0 / (trace / rows)
    system = system * unit + jnp.where(eye, 1.0, 0.0)
    system_halves = halves(system)
    first, steps = newton_plan(rows)
    inverse = jnp.where(eye, 2.0 * first * steps[0], 0.0) - (first * first * steps[0]) * system
    for scale in steps[1:]:
        inverse_halves = halves(inverse)
        residual = jnp.where(eye, 2.0, 0.0) - dot_halves(system_halves, inverse_halves)
        inverse = scale * dot_halves(inverse_halves, halves(residual))
    read.wait()
    write = pltpu.make_async_copy(root, root_out, sems.at[1])
    write.start()
    target = rhs_ref[...] * unit
    inverse_halves = halves(inverse)
    solved = dot_halves(halves(target), inverse_halves)
    for _ in range(2):
        solved = solved + dot_halves(halves(target - dot_high(solved, system)), inverse_halves)
    pre_out[...] = grads_ref[...] - dot_mid(solved, root[...])
    write.wait()


def fused_body(
    activations,
    out_grads,
    input_proj,
    grad_proj,
    example_count,
    child_order,
    prior_sketch,
    fold_map,
    merge_mix,
):
    n_dp, n_tp = lax.axis_size("dp"), lax.axis_size("tensor")
    rows, columns = prior_sketch.shape
    slots = activations.shape[0] // SEQ
    f32, bf16 = jnp.float32, jnp.bfloat16
    width, hidden = activations.shape[1], out_grads.shape[1]
    phases = 5
    hbm = pl.BlockSpec(memory_space=pl.ANY)
    vmem = pl.BlockSpec(memory_space=pltpu.VMEM)
    smem = pl.BlockSpec(memory_space=pltpu.SMEM)
    part_rows = -(-(rows // n_dp + slots) // 8) * 8
    root, gram, rhs, grads = pl.pallas_call(
        functools.partial(fused_kernel, n_dp, n_tp),
        out_shape=(
            jax.ShapeDtypeStruct((rows, columns), f32),
            jax.ShapeDtypeStruct((rows, rows), f32),
            jax.ShapeDtypeStruct((slots, rows), f32),
            jax.ShapeDtypeStruct((slots, columns), f32),
        ),
        in_specs=[hbm, hbm, hbm, hbm, smem, smem, hbm, vmem, vmem],
        out_specs=(hbm, vmem, vmem, vmem),
        scratch_shapes=[
            pltpu.VMEM((slots, SEQ, width), bf16),
            pltpu.VMEM((slots, SEQ, hidden), bf16),
            pltpu.VMEM((RANK, width), bf16),
            pltpu.VMEM((RANK, hidden), bf16),
            pltpu.VMEM((rows, columns), f32),
            pltpu.VMEM((n_dp // 2, rows, LANES), f32),
            pltpu.VMEM((n_dp // 2, rows, LANES), f32),
            pltpu.VMEM((n_dp // 2, rows, LANES), f32),
            pltpu.VMEM((2 * n_tp, SEQ, LANES), f32),
            pltpu.VMEM((n_tp, SEQ, LANES), f32),
            pltpu.VMEM((RANK, LANES), f32),
            pltpu.VMEM((n_tp, n_dp, LANES), f32),
            pltpu.VMEM((n_dp, n_tp, LANES), f32),
            pltpu.VMEM((n_dp, n_tp, LANES), f32),
            pltpu.VMEM((n_tp, 8, LANES), f32),
            pltpu.VMEM((n_dp, 8, LANES), f32),
            pltpu.VMEM((rows, columns), f32),
            pltpu.VMEM((n_dp, part_rows, rows), f32),
            pltpu.VMEM((n_dp, part_rows, rows), f32),
            pltpu.VMEM((n_tp, part_rows, rows), f32),
            pltpu.VMEM((rows, rows), f32),
            pltpu.SemaphoreType.DMA((3 + 2 * n_tp,)),
            pltpu.SemaphoreType.DMA((2, n_dp // 2)),
            pltpu.SemaphoreType.DMA((2, 3)),
            pltpu.SemaphoreType.DMA((2, 8)),
            pltpu.SemaphoreType.DMA((phases, n_tp)),
            pltpu.SemaphoreType.DMA((phases, n_tp)),
            pltpu.SemaphoreType.DMA((phases, n_dp)),
            pltpu.SemaphoreType.DMA((phases, n_dp)),
            pltpu.SemaphoreType.DMA((1,)),
        ],
        compiler_params=pltpu.CompilerParams(
            collective_id=0, has_side_effects=True, vmem_limit_bytes=56 * 2**20
        ),
    )(
        activations,
        out_grads,
        input_proj.T,
        grad_proj.T,
        example_count,
        child_order,
        prior_sketch,
        fold_map.T,
        merge_mix,
    )
    return pl.pallas_call(
        solve_kernel,
        out_shape=(
            jax.ShapeDtypeStruct((rows, columns), f32),
            jax.ShapeDtypeStruct((slots, columns), f32),
        ),
        in_specs=[hbm, vmem, vmem, vmem],
        out_specs=(hbm, vmem),
        scratch_shapes=[pltpu.VMEM((rows, columns), f32), pltpu.SemaphoreType.DMA((2,))],
        compiler_params=pltpu.CompilerParams(vmem_limit_bytes=56 * 2**20),
    )(root, gram, rhs, grads)


def from_partner(value, axis, stride):
    mask = 2**stride
    pairs = [(source, source ^ mask) for source in range(lax.axis_size(axis))]
    return lax.ppermute(value, axis, pairs)


def body(
    activations,
    out_grads,
    input_proj,
    grad_proj,
    example_count,
    child_order,
    prior_sketch,
    fold_map,
    merge_mix,
):
    tensor_count = lax.axis_size("tensor")
    own_rank = RANK // tensor_count
    example_slots = activations.shape[0] // SEQ
    sketch_rows = prior_sketch.shape[0]
    input_part = jnp.dot(activations, input_proj, preferred_element_type=jnp.float32)
    grad_part = jnp.dot(out_grads, grad_proj, preferred_element_type=jnp.float32)
    input_side, grad_side = lax.psum((input_part, grad_part), "tensor")
    grad_own = lax.dynamic_slice_in_dim(grad_side, lax.axis_index("tensor") * own_rank, own_rank, 1)
    grad_blocks = grad_own.reshape(example_slots, SEQ, own_rank)
    input_blocks = input_side.reshape(example_slots, SEQ, RANK)
    example_grad = jnp.einsum(
        "eta,etb->eab", grad_blocks, input_blocks, precision=lax.Precision.HIGHEST
    )
    example_grad = example_grad.reshape(example_slots, own_rank * RANK) / jnp.sqrt(jnp.float32(SEQ))
    live = jnp.arange(example_slots, dtype=jnp.int32) < example_count[0]
    example_grad = jnp.where(live[:, None], example_grad, jnp.zeros_like(example_grad))
    leaf_node = prior_sketch + jnp.dot(fold_map, example_grad, precision=lax.Precision.HIGHEST)
    leaf_weight = lax.psum(jnp.sum(leaf_node * leaf_node), "tensor")
    mix_first = merge_mix[:, :sketch_rows]
    mix_second = merge_mix[:, sketch_rows:]
    depth_count = lax.axis_size("dp").bit_length() - 1
    rank_index = lax.axis_index("dp")
    sketch_node = leaf_node
    sketch_weight = leaf_weight
    for level_index in range(depth_count):
        sibling_node, sibling_weight = from_partner((sketch_node, sketch_weight), "dp", level_index)
        upper_half = rank_index >> level_index & 1
        block_start = rank_index >> level_index + 1 << level_index + 1
        flip_order = child_order[block_start + (1 << level_index) - 1]
        own_first = upper_half == flip_order
        first = jnp.where(own_first, sketch_node, sibling_node)
        second = jnp.where(own_first, sibling_node, sketch_node)
        first_weight = jnp.where(own_first, sketch_weight, sibling_weight)
        second_weight = jnp.where(own_first, sibling_weight, sketch_weight)
        mixture = jnp.dot(mix_first, first, precision=lax.Precision.HIGHEST) + jnp.dot(
            mix_second, second, precision=lax.Precision.HIGHEST
        )
        mix_total = lax.psum(jnp.sum(mixture * mixture), "tensor")
        sketch_weight = first_weight + second_weight
        sketch_node = mixture * jnp.sqrt(sketch_weight / (mix_total + 1e-06))
    gram_part = jnp.dot(sketch_node, sketch_node.T, precision=lax.Precision.HIGHEST)
    product_part = jnp.dot(sketch_node, example_grad.T, precision=lax.Precision.HIGHEST)
    gram, sketch_grad = lax.psum((gram_part, product_part), "tensor")
    damping = jnp.trace(gram) / sketch_rows
    system = gram + damping * jnp.eye(sketch_rows, dtype=jnp.float32)
    factor = jnp.linalg.cholesky(system)
    solved = jax.scipy.linalg.cho_solve((factor, True), sketch_grad)
    preconditioned = example_grad - jnp.dot(solved.T, sketch_node, precision=lax.Precision.HIGHEST)
    return (sketch_node, preconditioned)


def fits_fused(rows, columns, slots, n_dp, n_tp):
    return (
        columns == n_dp * LANES
        and slots == n_tp
        and 2 * RANK == LANES
        and n_dp == 8
        and rows % (8 * n_dp) == 0
    )


def step(*args):
    n_dp, n_tp = lax.axis_size("dp"), lax.axis_size("tensor")
    slots = args[0].shape[0] // SEQ
    rows, columns = args[6].shape
    if fits_fused(rows, columns, slots, n_dp, n_tp):
        return fused_body(*args)
    return body(*args)


def solution(mesh):
    in_specs = (
        P("dp", "tensor"),
        P("dp", "tensor"),
        P("tensor", None),
        P("tensor", None),
        P("dp"),
        P(),
        P("dp", "tensor"),
        P(),
        P(),
    )
    out_specs = (P(None, "tensor"), P("dp", "tensor"))
    return jax.shard_map(step, mesh=mesh, in_specs=in_specs, out_specs=out_specs, check_vma=False)
```
